32 devices in a mesh: leaf: 2 (over y), user: 4 (over x, core), tensor: 4 (over z).
Axes of the slice: x: 2, y: 2, z: 4, core: 2. Of those that a mesh axis runs over, the one named last changes fastest.
Arguments:
- user_feat: bfloat16 [32, 128], P('user'), may hold values from -6 to 6
- beam_nodes: int32 [32, 128], P('user', ('leaf', 'tensor')), may hold values from 0 to 16383, as said below
- item_ids: int32 [32, 384], P('user', 'leaf'), may hold values from 0 to 16383, as said below
- subtree_slot: int32 [32], replicated, may hold values from 0 to 31, as said below
- node_table: bfloat16 [16384, 128], P(('leaf', 'tensor')), may hold values from -6 to 6
- item_table: bfloat16 [16384, 128], P(('leaf', 'tensor')), may hold values from -6 to 6
- mlp_user: bfloat16 [128, 1024], replicated, may hold values from -0.375 to 0.375
- mlp_node: bfloat16 [128, 1024], replicated, may hold values from -0.375 to 0.375
- mlp_bias: float32 [1024], replicated, may hold values from -3 to 3
- mlp_out: bfloat16 [1024], replicated, may hold values from -0.1875 to 0.1875
- proj_in: bfloat16 [384, 2048], P(None, 'tensor'), may hold values from -0.3125 to 0.3125
- cross_w: bfloat16 [2, 2048, 2048], P(None, None, 'tensor'), may hold values from -0.125 to 0.125
- cross_b: float32 [2, 2048], P(None, 'tensor'), may hold values from -3 to 3
- out_w: bfloat16 [2048], P('tensor'), may hold values from -0.125 to 0.125
Outputs:
- beam_score: float32 [32, 128], P('user', ('leaf', 'tensor'))
- interest: float32 [32, 128], P('user')
- logit: float32 [32, 384], P('user', 'leaf')
The draws below stay inside these ranges and needn't reach their ends.
Inputs may be any that keep to these rules, and one draw needn't show every extreme that they name: A permutation of the subtrees: subtree s is held by index subtree_slot[s] // 4 of leaf+tensor (leaf-major), as its block subtree_slot[s] % 4. `beam_nodes`: within the 8 x 16 block of one device, at most 16 nodes belong to subtrees held by any one index of leaf+tensor; some index receives exactly 16 from every device's block. `item_ids`: split a device's 8 x 192 block, flattened user by user, into 4 runs of 384 items; each run has at most 48 items of subtrees held by any one index of leaf+tensor, and some index receives exactly 48 from every run.
All inputs are finite; a program needn't handle non-finite values.
Results may differ from the reference program's by a relative error of at most 0.0062.
Values may be sent and summed in bfloat16 or wider, within the bound.
A program may use at most 64 MiB of HBM per device.

```python
import math
import jax
import jax.numpy as jnp
from jax import lax

E = 128
H = 1024
W = 2048
LAYERS = 2
SUB_NODES = 512
SUB_ITEMS = 512
SUB_DEV = 4
U_DEV = 8
BEAM_DEV = 16
ITEM_DEV = 192
USERS = 32
BEAM = 128
K = 384
NODES = 16384
ITEMS = 16384
CAP_B = 16
FETCH = 384
CAP_I = 48
N_LEAF = 2
N_USER = 4
N_TENSOR = 4


def slot_table(key):
    return jax.random.permutation(jax.random.fold_in(key, 7), SUB_DEV * N_LEAF * N_TENSOR).astype(jnp.int32)


def owner_blocks(key, blocks, per_block, owners, capacity):
    hot = jax.random.randint(jax.random.fold_in(key, 11), (), 0, owners)
    keys = jax.random.split(jax.random.fold_in(key, 12), blocks)

    def one_block(block_key):
        order_key, shuffle_key = jax.random.split(block_key)
        others = jax.random.permutation(order_key, owners - 1).astype(jnp.int32)
        place = jnp.arange(per_block, dtype=jnp.int32)
        spread = others[jnp.maximum(place - capacity, 0) % (owners - 1)]
        owner = jnp.where(place < capacity, hot, (hot + 1 + spread) % owners)
        return jax.random.permutation(shuffle_key, owner.astype(jnp.int32))
    return jax.vmap(one_block)(keys)


def ids_from_owners(key, salt, owner, span):
    slot_map = slot_table(key)
    subtree_of = jnp.argsort(slot_map).astype(jnp.int32)
    pick = jax.random.randint(jax.random.fold_in(key, salt + 1), owner.shape, 0, SUB_DEV)
    within = jax.random.randint(jax.random.fold_in(key, salt + 2), owner.shape, 0, span)
    subtree = subtree_of[owner * SUB_DEV + pick]
    return (subtree * span + within).astype(jnp.int32)


def draw_subtree_slot(key, part):
    return slot_table(key)


def draw_beam_nodes(key, part):
    owners = N_LEAF * N_TENSOR
    owner = owner_blocks(jax.random.fold_in(key, 100), N_USER * owners, U_DEV * BEAM_DEV, owners, CAP_B)
    ids = ids_from_owners(key, 100, owner, SUB_NODES)
    ids = ids.reshape(N_USER, owners, U_DEV, BEAM_DEV).transpose(0, 2, 1, 3)
    return ids.reshape(USERS, BEAM)


def draw_item_ids(key, part):
    owners = N_LEAF * N_TENSOR
    owner = owner_blocks(jax.random.fold_in(key, 200), N_USER * N_LEAF * N_TENSOR, FETCH, owners, CAP_I)
    ids = ids_from_owners(key, 200, owner, SUB_ITEMS)
    ids = ids.reshape(N_USER, N_LEAF, U_DEV, ITEM_DEV).transpose(0, 2, 1, 3)
    return ids.reshape(USERS, K)


def block_scale(key, extent, cuts, low, top_value):
    level = 1.0
    for axis_at, parts in cuts:
        steps = jax.random.uniform(jax.random.fold_in(jax.random.fold_in(key, 6), axis_at), (parts,), jnp.float32, low / len(cuts), top_value / len(cuts))
        level = level * jnp.repeat(jnp.exp(steps), extent[axis_at] // parts).reshape((-1,) + (1,) * (len(extent) - 1 - axis_at))
    return level


def gaussian(own_key, extent, width, limit, cuts=(), kind=jnp.bfloat16):
    values = width * jax.random.normal(own_key, extent, jnp.float32)
    if cuts:
        values = values * block_scale(own_key, extent, cuts, -0.22, 0.18)
    return jnp.clip(values, -limit, limit).astype(kind)


def setup_inputs(seed: int = 0) -> dict:
    arg_keys = jax.random.split(jax.random.key(seed), 15)
    return {
        "user_feat": gaussian(arg_keys[0], (USERS, E), 1.0, 6.0, ((0, 4),)),
        "beam_nodes": draw_beam_nodes(jax.random.fold_in(arg_keys[14], 71), 0),
        "item_ids": draw_item_ids(jax.random.fold_in(arg_keys[14], 71), 0),
        "subtree_slot": draw_subtree_slot(jax.random.fold_in(arg_keys[14], 71), 0),
        "node_table": gaussian(arg_keys[4], (NODES, E), 1.0, 6.0, ((0, 8),)),
        "item_table": gaussian(arg_keys[5], (ITEMS, E), 1.0, 6.0, ((0, 8),)),
        "mlp_user": gaussian(arg_keys[6], (E, H), (2 * E) ** -0.5, 0.375),
        "mlp_node": gaussian(arg_keys[7], (E, H), (2 * E) ** -0.5, 0.375),
        "mlp_bias": gaussian(arg_keys[8], (H,), 0.5, 3.0, (), jnp.float32),
        "mlp_out": gaussian(arg_keys[9], (H,), H ** -0.5, 0.1875),
        "proj_in": gaussian(arg_keys[10], (3 * E, W), (3 * E) ** -0.5, 0.3125, ((1, 4),)),
        "cross_w": gaussian(arg_keys[11], (LAYERS, W, W), W ** -0.5, 0.125, ((2, 4),)),
        "cross_b": gaussian(arg_keys[12], (LAYERS, W), 0.5, 3.0, ((1, 4),), jnp.float32),
        "out_w": gaussian(arg_keys[13], (W,), W ** -0.5, 0.125, ((0, 4),)),
    }


def reference(user_feat, beam_nodes, item_ids, subtree_slot, node_table, item_table, mlp_user, mlp_node, mlp_bias, mlp_out, proj_in, cross_w, cross_b, out_w):
    node_row = subtree_slot[beam_nodes // SUB_NODES] * SUB_NODES + beam_nodes % SUB_NODES
    node_vec = node_table[node_row]
    user_part = jnp.dot(user_feat, mlp_user, preferred_element_type=jnp.float32)
    node_part = jnp.dot(node_vec.reshape(USERS * BEAM, E), mlp_node, preferred_element_type=jnp.float32).reshape(USERS, BEAM, H)
    hidden = jax.nn.silu(user_part[:, None, :] + node_part + mlp_bias).astype(jnp.bfloat16)
    beam_score = jnp.dot(hidden.reshape(USERS * BEAM, H), mlp_out, preferred_element_type=jnp.float32).reshape(USERS, BEAM)
    weights = jax.nn.sigmoid(beam_score)
    interest = jnp.einsum('ub,ube->ue', weights, node_vec.astype(jnp.float32), precision=lax.Precision.HIGHEST) / math.sqrt(BEAM)
    item_row = subtree_slot[item_ids // SUB_ITEMS] * SUB_ITEMS + item_ids % SUB_ITEMS
    item_vec = item_table[item_row]
    interest_b = interest.astype(jnp.bfloat16)
    user_cols = jnp.broadcast_to(user_feat[:, None, :], (USERS, K, E))
    interest_cols = jnp.broadcast_to(interest_b[:, None, :], (USERS, K, E))
    inputs = jnp.concatenate([user_cols, interest_cols, item_vec], axis=2).reshape(USERS * K, 3 * E)
    x_first = jnp.dot(inputs, proj_in, preferred_element_type=jnp.float32).astype(jnp.bfloat16)
    x_now = x_first
    for layer in range(LAYERS):
        mixed = jnp.dot(x_now, cross_w[layer], preferred_element_type=jnp.float32) + cross_b[layer]
        x_now = (x_first.astype(jnp.float32) * mixed + x_now.astype(jnp.float32)).astype(jnp.bfloat16)
    logit = jnp.dot(x_now, out_w, preferred_element_type=jnp.float32).reshape(USERS, K)
    return (beam_score, interest, logit)
```

```python
import functools
import math

import jax
import jax.numpy as jnp
from jax import lax
from jax.experimental import pallas as pl
from jax.experimental.pallas import tpu as pltpu
from jax.sharding import PartitionSpec as P

SUB_NODES = 512
SUB_ITEMS = 512
BOTH = ("leaf", "tensor")
F32 = jnp.float32
BF16 = jnp.bfloat16
I32 = jnp.int32
LANES = 128


def dot(left, right):
    return jnp.dot(left, right, preferred_element_type=F32)


def dot_nt(left, right):
    return lax.dot_general(left, right, (((1,), (1,)), ((), ())), preferred_element_type=F32)


def split(x):
    high = x.astype(BF16)
    return jnp.concatenate([high, (x - high.astype(F32)).astype(BF16)], axis=0)


def iota(shape, axis):
    return lax.broadcasted_iota(I32, shape, axis)


def ones_where(mask):
    return jnp.where(mask, 1.0, 0.0).astype(BF16)


def log2(n):
    assert n & (n - 1) == 0
    return n.bit_length() - 1


def kernel(
    cfg, uf_h, beam_h, item_h, slot_h, node_h, itab_h, mu_h, mn_h, mb_h, mo_h, proj_h, cw_h, cb_h, ow_h,
    score_o, interest_o, logit_o,
    uf, beam, ids, slots, node, itab, mu, mlp, mb, mo, proj, cw, cb, ow, in_sem,
    brow, rows, arr, pbuf, sout, sin, abuf, qout, qin, pall, fall, ppo, ppi, qall, lk, hot, lbuf,
    b_s, b_r, i_s, i_r, p_s, p_r, r_s, r_r, n_s, n_r, c_s, c_r, a_s, a_r, u_s, u_r, f_s, f_r, w_s, w_r, q_s, q_r, l_s, l_r,
):
    leafs, tensors, user_count, upr, cap_i, cap_b, per_n, per_i, split_leaf = cfg
    leaf, tensor, user = (lax.axis_index(a) for a in ("leaf", "tensor", "user"))
    owners = leafs * tensors
    me = leaf * tensors + tensor
    users, items = ids.shape[1:]
    width = uf.shape[1]
    two = 2 * width
    cols = proj.shape[1]
    beams = beam.shape[1]
    spots = users * beams
    groups = users // upr
    hidden_n = mu.shape[1]
    pleafs = leafs if split_leaf else 1
    pieces = pleafs * user_count
    piece = user * pleafs + (leaf if split_leaf else 0)
    prow = width // pieces

    def wide(k):
        kl, kt = k // tensors, k % tensors
        return {"leaf": (leaf + kl) % leafs, "tensor": (tensor + kt) % tensors}

    def along(k):
        return {"tensor": (tensor + k) % tensors}

    def across(k):
        return {"leaf": (leaf + k) % leafs}

    def same(k):
        if not split_leaf:
            return {"user": (user + k) % user_count}
        ku, kl = k // pleafs, k % pleafs
        return {"user": (user + ku) % user_count, "leaf": (leaf + kl) % leafs}

    def remote(src, dst, ssem, rsem, k, who):
        return pltpu.make_async_remote_copy(
            src_ref=src, dst_ref=dst, send_sem=ssem.at[k - 1], recv_sem=rsem.at[k - 1],
            device_id=who(k), device_id_type=pl.DeviceIdType.MESH,
        )

    def each(first, last, make, what):
        @pl.loop(first, last)
        def _(k):
            getattr(make(k), what)()

    loads = {}

    def load(name, src, dst):
        loads[name] = pltpu.make_async_copy(src, dst, in_sem.at[len(loads)])
        loads[name].start()

    load("slots", slot_h, slots)
    load("beam", beam_h, beam)
    load("ids", item_h, ids.at[leaf])
    load("proj", proj_h, proj)
    load("itab", itab_h, itab)
    load("uf", uf_h, uf)
    load("mu", mu_h, mu)
    load("mn", mn_h, mlp.at[pl.ds(0, width)])
    load("mb", mb_h, mb)
    load("mo", mo_h, mo)
    load("node", node_h, node)
    load("w1", cw_h.at[1], cw.at[1])
    load("w0", cw_h.at[0], cw.at[0])
    load("cb", cb_h, cb)
    load("ow", ow_h, ow)

    barrier = pltpu.get_barrier_semaphore()

    def greet(who):
        def one(k):
            pl.semaphore_signal(barrier, inc=1, device_id=who(k), device_id_type=pl.DeviceIdType.MESH)
        return one

    pl.loop(1, owners)(greet(wide))
    pl.loop(pleafs, pieces)(greet(same))

    loads["beam"].wait()
    spread = jnp.concatenate([beam[...], jnp.zeros((users, spots - beams), I32)], axis=1)
    spread = pltpu.roll(spread, 0, axis=1, stride=beams, stride_axis=0)
    mine = iota((users, spots), 1) // beams == iota((users, spots), 0)
    brow[me] = jnp.sum(jnp.where(mine, spread, 0), axis=0, keepdims=True)
    loads["ids"].wait()
    loads["proj"].wait()
    pall[tensor] = proj[pl.ds(pl.multiple_of(two + piece * prow, prow), prow), :]

    pl.semaphore_wait(barrier, owners - 1 + pieces - pleafs)

    def item_copy(k):
        return remote(ids.at[leaf], ids.at[leaf], i_s, i_r, k, across)

    def beam_copy(k):
        return remote(brow.at[me], brow.at[me], b_s, b_r, k, wide)

    def proj_copy(k):
        return remote(pall.at[tensor], pall.at[tensor], p_s, p_r, k, along)

    each(1, owners, beam_copy, "start")
    each(1, leafs, item_copy, "start")
    each(1, tensors, proj_copy, "start")

    loads["slots"].wait()
    n_sub = slots.shape[0]

    def locate(at, span, per):
        sub = at >> log2(span)

        def one(s, slot):
            return jnp.where(sub == s, slots[s], slot)

        slot = lax.fori_loop(0, n_sub, one, jnp.zeros_like(at), unroll=min(n_sub, 32))
        return slot >> log2(per), ((slot & (per - 1)) << log2(span)) + (at & (span - 1))

    before = ones_where(iota((items, items), 0) < iota((items, items), 1))
    alls = jnp.ones((items, items), BF16)

    def rank_of(marks):
        n = marks.shape[0]
        r, c = iota((n, n), 0), iota((n, n), 1)
        earlier = ones_where((r // upr == c // upr) & (c < r))
        return dot(marks, before) + dot(earlier, dot(marks, alls).astype(BF16))

    def pick(table, wanted):
        n, total = wanted.shape[0], table.shape[0]
        step = min(total, 512)
        out = jnp.zeros((n, width), F32)
        for at in range(0, total, step):
            hit = ones_where(wanted - at == iota((n, step), 1))
            out = out + dot(hit, table[at : at + step, :])
        return out.astype(BF16)

    def chosen_items(rank, local):
        s = iota((cap_i, items), 0)
        lists = []
        for g in range(groups):
            total = jnp.zeros((cap_i, items), I32)
            for u in range(g * upr, (g + 1) * upr):
                total = total + jnp.where(rank[u : u + 1, :] == s, local[u : u + 1, :] + 1, 0)
            lists.append(jnp.sum(total, axis=1, keepdims=True) - 1)
        return pick(itab, jnp.concatenate(lists, axis=0))

    own_owner, own_local = locate(ids[leaf], SUB_ITEMS, per_i)
    marks3 = own_owner[None] == iota((owners, users, items), 0)
    ranks3 = rank_of(ones_where(marks3).reshape(owners * users, items)).reshape(owners, users, items)
    own_rank = jnp.sum(jnp.where(marks3, ranks3, 0.0), axis=0).astype(I32)
    loads["itab"].wait()
    picked = chosen_items(jnp.where(own_owner == me, own_rank, -1), own_local)
    rows[leaf] = picked
    arr[me] = picked

    def rows_copy(k):
        return remote(rows.at[(leaf + k // tensors) % leafs], arr.at[me], r_s, r_r, k, wide)

    each(1, tensors, rows_copy, "start")

    for name in ("uf", "mu", "mb", "mn", "mo"):
        loads[name].wait()
    up = dot(uf[...], mu[...]) + mb[...].reshape(1, hidden_n)
    mlp[width : width + 2 * users, :] = split(up)
    mlp[width + 2 * users :, :] = jnp.zeros((width - 2 * users, hidden_n), BF16)
    shared_lane = iota((1, width), 1)
    pair_lane = shared_lane < 2 * users
    user_lane = shared_lane & (users - 1)

    each(1, owners, beam_copy, "wait_recv")
    n_owner, n_local = locate(brow[:, 0, :], SUB_NODES, per_n)
    n_mark = n_owner == me
    n_rank = dot(ones_where(n_mark), ones_where(iota((spots, spots), 0) < iota((spots, spots), 1)))
    n_rank = jnp.where(n_mark, n_rank.astype(I32), -1)
    coded = n_local * users + iota((owners, spots), 1) // beams + 1
    n_hit = n_rank[:, None, :] == iota((owners, cap_b, spots), 1)
    places = owners * cap_b
    code = jnp.sum(jnp.where(n_hit, coded[:, None, :], 0), axis=2, keepdims=True).reshape(places, 1) - 1
    loads["node"].wait()
    node_rows = pick(node, code >> log2(users))
    user_hot = (code >= 0) & ((code & (users - 1)) == user_lane) & pair_lane
    left = jnp.concatenate([node_rows, ones_where(user_hot)], axis=1)
    step = min(hidden_n, 256)
    score = jnp.zeros((users, places), F32)
    out_row = jnp.broadcast_to(mo[...].reshape(1, hidden_n), (users, hidden_n))
    for at in range(0, hidden_n, step):
        half = 0.5 * dot(left, mlp[:, at : at + step])
        hidden = (half + half * jnp.tanh(half)).astype(BF16)
        score = score + dot_nt(out_row[:, at : at + step], hidden)
    gate = 0.5 + 0.5 * jnp.tanh(0.5 * score)
    gate = gate * jnp.transpose(jnp.where(user_hot, 1.0, 0.0))[:users, :]
    sums = dot(split(gate), node_rows)
    pbuf[me] = sums[:users] + sums[users:]

    def sums_copy(k):
        return remote(pbuf.at[me], pbuf.at[me], n_s, n_r, k, wide)

    each(1, owners, sums_copy, "start")

    def other_leaf(k):
        item_copy(k).wait_recv()
        their = (leaf + leafs - k) % leafs
        owner, local = locate(ids[their], SUB_ITEMS, per_i)
        mark = owner == me
        rank = rank_of(ones_where(mark)).astype(I32)
        rows[their] = chosen_items(jnp.where(mark, rank, -1), local)

    def their_rows(k):
        back = leafs - k
        return back * tensors, (back + 1) * tensors

    if leafs == 2:
        other_leaf(1)
        each(tensors, 2 * tensors, rows_copy, "start")
    else:

        @pl.loop(1, leafs)
        def _(k):
            other_leaf(k)
            first, last = their_rows(k)
            each(first, last, rows_copy, "start")

    own_lane = iota((owners, places), 1) // cap_b == iota((owners, places), 0)
    score_rows = jnp.where(own_lane, score[0:1, :], 0.0)
    back = dot(split(score_rows), ones_where(n_hit.reshape(places, spots)))
    sout[...] = (back[:owners] + back[owners:])[:, None, :]
    sin[me] = sout[me]

    def score_copy(k):
        to = wide(k)
        return remote(sout.at[to["leaf"] * tensors + to["tensor"]], sin.at[me], c_s, c_r, k, wide)

    each(1, owners, score_copy, "start")

    loads["ow"].wait()
    loads["cb"].wait()
    loads["w1"].wait()
    weight = ow[...].astype(F32).reshape(1, cols)

    def through_second(x):
        return dot_nt((x * weight).astype(BF16), cw[1])

    part = through_second(pall[tensor].astype(F32)).astype(BF16)
    for t in range(tensors):
        ppo[t] = part[:, t * cols : (t + 1) * cols]
    ppi[tensor] = ppo[tensor]

    def part_copy(k):
        to = (tensor + k) % tensors
        return remote(ppo.at[to], ppi.at[tensor], w_s, w_r, k, along)

    each(1, tensors, part_copy, "start")
    loads["w0"].wait()
    each(1, tensors, proj_copy, "wait_recv")

    def through_first(parts):
        total = jnp.zeros((parts.shape[1], cols), F32)
        for t in range(tensors):
            total = total + dot(parts[t].astype(BF16), cw[0, t * cols : (t + 1) * cols, :])
        return total

    fall[piece] = through_first(pall).astype(BF16)

    def first_copy(k):
        return remote(fall.at[piece], fall.at[piece], f_s, f_r, k, same)

    each(1, pieces, first_copy, "start")
    a_user = dot(uf[...], proj[:width, :])

    each(1, owners, sums_copy, "wait_recv")
    interest = jnp.sum(pbuf[...], axis=0) * (1.0 / math.sqrt(owners * beams))
    interest_o[...] = interest
    a_user = a_user + dot(interest.astype(BF16), proj[width:two, :])
    abuf[tensor] = a_user

    def a_copy(k):
        return remote(abuf.at[tensor], abuf.at[tensor], a_s, a_r, k, along)

    each(1, tensors, a_copy, "start")
    part = through_second(a_user)
    for t in range(tensors):
        qout[t] = part[:, t * cols : (t + 1) * cols]
    qin[tensor] = qout[tensor]

    def q_copy(k):
        to = (tensor + k) % tensors
        return remote(qout.at[to], qin.at[tensor], u_s, u_r, k, along)

    each(1, tensors, q_copy, "start")

    each(1, tensors, part_copy, "wait_recv")
    qall[piece] = jnp.sum(ppi[...].astype(F32), axis=0).astype(BF16)

    def second_copy(k):
        return remote(qall.at[piece], qall.at[piece], q_s, q_r, k, same)

    each(1, pieces, second_copy, "start")

    place = (own_owner * cap_i + own_rank).astype(F32)
    place = jnp.transpose(place).astype(I32)
    slots_n = owners * cap_i
    for u in range(users):
        hot[u] = ones_where(place[:, u : u + 1] == iota((items, slots_n), 1))
    lk[0:width, 0:cols] = proj[two:, :]
    lk[width + 2 * users :, :] = jnp.zeros((width - 2 * users, 3 * cols), BF16)

    each(1, owners, score_copy, "wait_recv")
    flat = jnp.sum(sin[...], axis=0)
    flat = jnp.broadcast_to(flat, (users, spots))
    by_user = flat
    for u in range(1, users):
        turned = pltpu.roll(flat, spots - u * beams, axis=1)
        by_user = jnp.where(iota((users, spots), 0) == u, turned, by_user)
    score_o[...] = by_user[:, :beams]

    each(1, tensors, a_copy, "wait_recv")
    h_user = through_first(abuf) + cb[0:1, :] + 1.0
    each(1, tensors, q_copy, "wait_recv")
    q_user = jnp.sum(qin[...], axis=0) + weight
    lk[width : width + 2 * users, :] = split(jnp.concatenate([a_user, h_user, q_user], axis=1))
    each(1, pieces, first_copy, "wait_recv")
    lk[0:width, cols : 2 * cols] = fall[...].reshape(width, cols)
    each(1, pieces, second_copy, "wait_recv")
    lk[0:width, 2 * cols :] = qall[...].reshape(width, cols)

    each(1, owners, rows_copy, "wait_recv")
    last = weight * cb[1:2, :]
    n = upr * items
    half = min(cols, 256)
    logit = jnp.zeros((users, items), F32)
    for g in range(groups):
        got = arr[:, g * cap_i : (g + 1) * cap_i, :].reshape(slots_n, width)
        vec = dot(hot[g * upr : (g + 1) * upr].reshape(n, slots_n), got).astype(BF16)
        who = g * upr + iota((n, width), 0) // items
        z = jnp.concatenate([vec, ones_where((who == user_lane) & pair_lane)], axis=1)
        total = jnp.zeros((n, LANES), F32)
        for at in range(0, cols, half):
            x0 = dot(z, lk[:, at : at + half])
            mixed = dot(z, lk[:, cols + at : cols + at + half])
            second = dot(z, lk[:, 2 * cols + at : 2 * cols + at + half])
            term = x0 * (mixed * second + last[:, at : at + half])
            for j in range(0, half, LANES):
                total = total + term[:, j : j + LANES]
        high = total.astype(BF16)
        low = (total - high.astype(F32)).astype(BF16)
        for u in range(upr):
            line = ones_where(iota((users, LANES), 0) == g * upr + u)
            held = slice(u * items, (u + 1) * items)
            logit = logit + dot_nt(line, high[held]) + dot_nt(line, low[held])
    lbuf[tensor] = logit

    def logit_copy(k):
        return remote(lbuf.at[tensor], lbuf.at[tensor], l_s, l_r, k, along)

    each(1, tensors, logit_copy, "start")
    each(1, owners, beam_copy, "wait_send")
    each(1, leafs, item_copy, "wait_send")
    each(1, tensors, proj_copy, "wait_send")
    each(1, owners, rows_copy, "wait_send")
    each(1, owners, sums_copy, "wait_send")
    each(1, owners, score_copy, "wait_send")
    each(1, tensors, part_copy, "wait_send")
    each(1, pieces, first_copy, "wait_send")
    each(1, tensors, a_copy, "wait_send")
    each(1, tensors, q_copy, "wait_send")
    each(1, pieces, second_copy, "wait_send")
    each(1, tensors, logit_copy, "wait")
    logit_o[...] = jnp.sum(lbuf[...], axis=0)


def per_device(*args):
    (user_feat, beam_nodes, item_ids, subtree_slot, node_table, item_table, mlp_user, mlp_node, mlp_bias, mlp_out,
     proj_in, cross_w, cross_b, out_w) = args
    leafs, tensors, user_count = (lax.axis_size(a) for a in ("leaf", "tensor", "user"))
    owners = leafs * tensors
    users, beams = beam_nodes.shape
    items = item_ids.shape[1]
    width = user_feat.shape[1]
    hidden_n = mlp_user.shape[1]
    cols = proj_in.shape[1]
    spots = users * beams
    cap_b = -(-max(2, -(-spots // owners)) // 8) * 8
    fetch = users * items // tensors
    cap_run = max(2, -(-fetch // owners))
    upr = next(
        u for u in range(1, users + 1)
        if users % u == 0 and u * items % fetch == 0 and (u * items // fetch * cap_run % 16 == 0 or u == users)
    )
    cap_i = upr * items // fetch * cap_run
    groups = users // upr
    split_leaf = width % (leafs * user_count * 16) == 0
    pieces = user_count * (leafs if split_leaf else 1)
    prow = width // pieces
    cfg = (
        leafs, tensors, user_count, upr, cap_i, cap_b,
        node_table.shape[0] // SUB_NODES, item_table.shape[0] // SUB_ITEMS, split_leaf,
    )
    vmem = pltpu.VMEM
    dma = pltpu.SemaphoreType.DMA
    scratch = [
        vmem(user_feat.shape, BF16),
        vmem(beam_nodes.shape, I32),
        vmem((leafs, users, items), I32),
        pltpu.SMEM(subtree_slot.shape, I32),
        vmem(node_table.shape, BF16),
        vmem(item_table.shape, BF16),
        vmem(mlp_user.shape, BF16),
        vmem((2 * width, hidden_n), BF16),
        vmem(mlp_bias.shape, F32),
        vmem(mlp_out.shape, BF16),
        vmem(proj_in.shape, BF16),
        vmem(cross_w.shape, BF16),
        vmem(cross_b.shape, F32),
        vmem(out_w.shape, BF16),
        dma((15,)),
        vmem((owners, 1, spots), I32),
        vmem((leafs, groups * cap_i, width), BF16),
        vmem((owners, groups * cap_i, width), BF16),
        vmem((owners, users, width), F32),
        vmem((owners, 1, spots), F32),
        vmem((owners, 1, spots), F32),
        vmem((tensors, users, cols), F32),
        vmem((tensors, users, cols), F32),
        vmem((tensors, users, cols), F32),
        vmem((tensors, prow, cols), BF16),
        vmem((pieces, prow, cols), BF16),
        vmem((tensors, prow, cols), BF16),
        vmem((tensors, prow, cols), BF16),
        vmem((pieces, prow, cols), BF16),
        vmem((2 * width, 3 * cols), BF16),
        vmem((users, items, owners * cap_i), BF16),
        vmem((tensors, users, items), F32),
    ]
    for n in (owners, leafs, tensors, owners, owners, owners, tensors, tensors, pieces, tensors, pieces, tensors):
        scratch += [dma((n - 1,))] * 2
    spec = pl.BlockSpec(memory_space=pltpu.VMEM)
    return pl.pallas_call(
        functools.partial(kernel, cfg),
        out_shape=(
            jax.ShapeDtypeStruct((users, beams), F32),
            jax.ShapeDtypeStruct((users, width), F32),
            jax.ShapeDtypeStruct((users, items), F32),
        ),
        in_specs=[pl.BlockSpec(memory_space=pl.ANY)] * len(args),
        out_specs=(spec, spec, spec),
        scratch_shapes=scratch,
        compiler_params=pltpu.CompilerParams(
            collective_id=0, has_side_effects=True, vmem_limit_bytes=56 << 20
        ),
    )(*args)


def solution(mesh):
    placed = (
        P("user", None),
        P("user", BOTH),
        P("user", "leaf"),
        P(),
        P(BOTH, None),
        P(BOTH, None),
        P(),
        P(),
        P(),
        P(),
        P(None, "tensor"),
        P(None, None, "tensor"),
        P(None, "tensor"),
        P("tensor"),
    )
    return jax.shard_map(
        per_device,
        mesh=mesh,
        in_specs=placed,
        out_specs=(P("user", BOTH), P("user", None), P("user", "leaf")),
        check_vma=False,
    )
```

```python
import functools
import math

import jax
import jax.numpy as jnp
from jax import lax
from jax.experimental import pallas as pl
from jax.experimental.pallas import tpu as pltpu
from jax.sharding import PartitionSpec as P

SUB_NODES = 512
SUB_ITEMS = 512
BOTH = ("leaf", "tensor")
F32 = jnp.float32
BF16 = jnp.bfloat16
I32 = jnp.int32
LANES = 128


def dot(left, right):
    return jnp.dot(left, right, preferred_element_type=F32)


def dot_nt(left, right):
    return lax.dot_general(left, right, (((1,), (1,)), ((), ())), preferred_element_type=F32)


def split(x):
    high = x.astype(BF16)
    return jnp.concatenate([high, (x - high.astype(F32)).astype(BF16)], axis=0)


def iota(shape, axis):
    return lax.broadcasted_iota(I32, shape, axis)


def ones_where(mask):
    return jnp.where(mask, 1.0, 0.0).astype(BF16)


def log2(n):
    assert n & (n - 1) == 0
    return n.bit_length() - 1


def kernel(
    cfg, uf_h, beam_h, item_h, slot_h, node_h, itab_h, mu_h, mn_h, mb_h, mo_h, proj_h, cw_h, cb_h, ow_h,
    score_o, interest_o, logit_o,
    uf, beam, ids, slots, node, itab, mu, mlp, mb, mo, proj, cw, cb, ow, in_sem,
    brow, rows, arr, pbuf, sout, sin, abuf, qout, qin, pall, fall, ppo, ppi, qall, lk, hot, lbuf,
    b_s, b_r, i_s, i_r, p_s, p_r, r_s, r_r, n_s, n_r, c_s, c_r, a_s, a_r, u_s, u_r, f_s, f_r, w_s, w_r, q_s, q_r, l_s, l_r,
):
    leafs, tensors, user_count, upr, cap_i, cap_b, per_n, per_i, split_leaf = cfg
    leaf, tensor, user = (lax.axis_index(a) for a in ("leaf", "tensor", "user"))
    owners = leafs * tensors
    me = leaf * tensors + tensor
    users, items = ids.shape[1:]
    width = uf.shape[1]
    two = 2 * width
    cols = proj.shape[1]
    beams = beam.shape[1]
    spots = users * beams
    groups = users // upr
    hidden_n = mu.shape[1]
    pleafs = leafs if split_leaf else 1
    pieces = pleafs * user_count
    piece = user * pleafs + (leaf if split_leaf else 0)
    prow = 2 * width // pieces

    def wrap(at, n):
        return at & (n - 1) if n & (n - 1) == 0 else at % n

    def wide(k):
        kl, kt = k // tensors, k % tensors
        return {"leaf": wrap(leaf + kl, leafs), "tensor": wrap(tensor + kt, tensors)}

    def along(k):
        return {"tensor": wrap(tensor + k, tensors)}

    def across(k):
        return {"leaf": wrap(leaf + k, leafs)}

    def same(k):
        if not split_leaf:
            return {"user": wrap(user + k, user_count)}
        ku, kl = k // pleafs, k % pleafs
        return {"user": wrap(user + ku, user_count), "leaf": wrap(leaf + kl, leafs)}

    def remote(src, dst, ssem, rsem, k, who):
        return pltpu.make_async_remote_copy(
            src_ref=src, dst_ref=dst, send_sem=ssem.at[k - 1], recv_sem=rsem.at[k - 1],
            device_id=who(k), device_id_type=pl.DeviceIdType.MESH,
        )

    def loop(first, last, one):
        if isinstance(first, int) and last - first <= 8:
            for k in range(first, last):
                one(k)
        else:
            pl.loop(first, last)(one)

    def each(first, last, make, what):
        loop(first, last, lambda k: getattr(make(k), what)())

    loads = {}

    def load(name, src, dst):
        loads[name] = pltpu.make_async_copy(src, dst, in_sem.at[len(loads)])
        loads[name].start()

    load("slots", slot_h, slots)
    load("beam", beam_h, beam)
    load("ids", item_h, ids.at[leaf])
    load("proj", proj_h, proj)
    load("uf", uf_h, uf)
    load("itab", itab_h, itab)
    load("mu", mu_h, mu)
    load("mn", mn_h, mlp.at[pl.ds(0, width)])
    load("mb", mb_h, mb)
    load("mo", mo_h, mo)
    load("node", node_h, node)
    load("ow", ow_h, ow)
    load("w1", cw_h.at[1], cw.at[1])
    load("cb", cb_h, cb)
    load("w0", cw_h.at[0], cw.at[0])

    def fold(x):
        return jnp.concatenate([x[:, : cols // 2], x[:, cols // 2 :]], axis=0).astype(BF16)

    def unfold(x):
        return jnp.concatenate([x[:users], x[users:]], axis=1)

    barrier = pltpu.get_barrier_semaphore()

    def greet(who):
        def one(k):
            pl.semaphore_signal(barrier, inc=1, device_id=who(k), device_id_type=pl.DeviceIdType.MESH)
        return one

    loop(1, owners, greet(wide))
    loop(pleafs, pieces, greet(same))

    loads["beam"].wait()
    spread = jnp.concatenate([beam[...], jnp.zeros((users, spots - beams), I32)], axis=1)
    spread = pltpu.roll(spread, 0, axis=1, stride=beams, stride_axis=0)
    mine = iota((users, spots), 1) // beams == iota((users, spots), 0)
    brow[me] = jnp.sum(jnp.where(mine, spread, 0), axis=0, keepdims=True)
    loads["ids"].wait()
    loads["proj"].wait()
    pall[tensor] = proj[pl.ds(pl.multiple_of(width + piece * prow, prow), prow), :]
    loads["uf"].wait()
    a_user = dot(uf[...], proj[:width, :])
    abuf[tensor] = fold(a_user)

    pl.semaphore_wait(barrier, owners - 1 + pieces - pleafs)

    def item_copy(k):
        return remote(ids.at[leaf], ids.at[leaf], i_s, i_r, k, across)

    def beam_copy(k):
        return remote(brow.at[me], brow.at[me], b_s, b_r, k, wide)

    def proj_copy(k):
        return remote(pall.at[tensor], pall.at[tensor], p_s, p_r, k, along)

    def a_copy(k):
        return remote(abuf.at[tensor], abuf.at[tensor], a_s, a_r, k, along)

    each(1, owners, beam_copy, "start")
    each(1, leafs, item_copy, "start")
    each(1, tensors, proj_copy, "start")
    each(1, tensors, a_copy, "start")

    loads["slots"].wait()
    n_sub = slots.shape[0]

    def locate(at, span, per):
        sub = at >> log2(span)

        def one(s, slot):
            return jnp.where(sub == s, slots[s], slot)

        slot = lax.fori_loop(0, n_sub, one, jnp.zeros_like(at), unroll=min(n_sub, 32))
        return slot >> log2(per), ((slot & (per - 1)) << log2(span)) + (at & (span - 1))

    before = ones_where(iota((items, items), 0) < iota((items, items), 1))
    alls = jnp.ones((items, items), BF16)

    def rank_of(marks):
        n = marks.shape[0]
        r, c = iota((n, n), 0), iota((n, n), 1)
        earlier = ones_where((r // upr == c // upr) & (c < r))
        return dot(marks, before) + dot(earlier, dot(marks, alls).astype(BF16))

    def pick(table, wanted):
        n, total = wanted.shape[0], table.shape[0]
        step = min(total, 512)
        out = jnp.zeros((n, width), F32)
        for at in range(0, total, step):
            hit = ones_where(wanted - at == iota((n, step), 1))
            out = out + dot(hit, table[at : at + step, :])
        return out.astype(BF16)

    def chosen_items(rank, local):
        s = iota((cap_i, items), 0)
        lists = []
        for g in range(groups):
            total = jnp.zeros((cap_i, items), I32)
            for u in range(g * upr, (g + 1) * upr):
                total = total + jnp.where(rank[u : u + 1, :] == s, local[u : u + 1, :] + 1, 0)
            lists.append(jnp.sum(total, axis=1, keepdims=True) - 1)
        return pick(itab, jnp.concatenate(lists, axis=0))

    loads["ow"].wait()
    loads["w1"].wait()
    weight = ow[...].astype(F32).reshape(1, cols)
    left = jnp.concatenate([pall[tensor].astype(F32), a_user], axis=0) * weight
    part = dot_nt(left.astype(BF16), cw[1])
    for t in range(tensors):
        held = part[:, t * cols : (t + 1) * cols]
        ppo[t] = held[:prow].astype(BF16)
        qout[t] = fold(held[prow:])
    ppi[tensor] = ppo[tensor]
    qin[tensor] = qout[tensor]

    def part_copy(k):
        return remote(ppo.at[wrap(tensor + k, tensors)], ppi.at[tensor], w_s, w_r, k, along)

    def q_copy(k):
        return remote(qout.at[wrap(tensor + k, tensors)], qin.at[tensor], u_s, u_r, k, along)

    each(1, tensors, part_copy, "start")
    each(1, tensors, q_copy, "start")

    own_owner, own_local = locate(ids[leaf], SUB_ITEMS, per_i)
    marks3 = own_owner[None] == iota((owners, users, items), 0)
    ranks3 = rank_of(ones_where(marks3).reshape(owners * users, items)).reshape(owners, users, items)
    own_rank = jnp.sum(jnp.where(marks3, ranks3, 0.0), axis=0).astype(I32)
    loads["itab"].wait()
    picked = chosen_items(jnp.where(own_owner == me, own_rank, -1), own_local)
    rows[leaf] = picked
    arr[me] = picked

    halves = 2 if groups % 2 == 0 else 1
    held_rows = groups * cap_i // halves

    def rows_copy(h):
        part = pl.ds(h * held_rows, held_rows)

        def one(k):
            return remote(
                rows.at[wrap(leaf + k // tensors, leafs), part], arr.at[me, part],
                r_s.at[h], r_r.at[h], k, wide,
            )
        return one

    each(1, tensors, rows_copy(0), "start")

    for name in ("mu", "mb", "mn", "mo"):
        loads[name].wait()
    up = dot(uf[...], mu[...]) + mb[...].reshape(1, hidden_n)
    mlp[width : width + 2 * users, :] = split(up)
    mlp[width + 2 * users :, :] = jnp.zeros((width - 2 * users, hidden_n), BF16)
    shared_lane = iota((1, width), 1)
    pair_lane = shared_lane < 2 * users
    user_lane = shared_lane & (users - 1)

    each(1, owners, beam_copy, "wait_recv")
    n_owner, n_local = locate(brow[:, 0, :], SUB_NODES, per_n)
    n_mark = n_owner == me
    n_rank = dot(ones_where(n_mark), ones_where(iota((spots, spots), 0) < iota((spots, spots), 1)))
    n_rank = jnp.where(n_mark, n_rank.astype(I32), -1)
    coded = n_local * users + iota((owners, spots), 1) // beams + 1
    n_hit = n_rank[:, None, :] == iota((owners, cap_b, spots), 1)
    places = owners * cap_b
    code = jnp.sum(jnp.where(n_hit, coded[:, None, :], 0), axis=2, keepdims=True).reshape(places, 1) - 1
    loads["node"].wait()
    node_rows = pick(node, code >> log2(users))
    user_hot = (code >= 0) & ((code & (users - 1)) == user_lane) & pair_lane
    left = jnp.concatenate([node_rows, ones_where(user_hot)], axis=1)
    step = min(hidden_n, 256)
    score = jnp.zeros((users, places), F32)
    out_row = jnp.broadcast_to(mo[...].reshape(1, hidden_n), (users, hidden_n))
    for at in range(0, hidden_n, step):
        half = 0.5 * dot(left, mlp[:, at : at + step])
        hidden = (half + half * jnp.tanh(half)).astype(BF16)
        score = score + dot_nt(out_row[:, at : at + step], hidden)
    gate = 0.5 + 0.5 * jnp.tanh(0.5 * score)
    gate = gate * jnp.transpose(jnp.where(user_hot, 1.0, 0.0))[:users, :]
    sums = dot(split(gate), node_rows)
    pbuf[me] = sums[:users] + sums[users:]

    def sums_copy(k):
        return remote(pbuf.at[me], pbuf.at[me], n_s, n_r, k, wide)

    each(1, owners, sums_copy, "start")

    own_lane = iota((owners, places), 1) // cap_b == iota((owners, places), 0)
    score_rows = jnp.where(own_lane, score[0:1, :], 0.0)
    back = dot(split(score_rows), ones_where(n_hit.reshape(places, spots)))
    sout[...] = (back[:owners] + back[owners:])[:, None, :]
    sin[me] = sout[me]

    def score_copy(k):
        to = wide(k)
        return remote(sout.at[to["leaf"] * tensors + to["tensor"]], sin.at[me], c_s, c_r, k, wide)

    each(1, owners, score_copy, "start")

    loads["w0"].wait()
    loads["cb"].wait()
    each(1, tensors, proj_copy, "wait_recv")
    each(1, tensors, a_copy, "wait_recv")
    total = jnp.zeros((prow + users, cols), F32)
    for t in range(tensors):
        left = jnp.concatenate([pall[t], unfold(abuf[t])], axis=0)
        total = total + dot(left, cw[0, t * cols : (t + 1) * cols, :])
    fall[piece] = total[:prow].astype(BF16)
    h_user = total[prow:] + cb[0:1, :] + 1.0

    def first_copy(k):
        return remote(fall.at[piece], fall.at[piece], f_s, f_r, k, same)

    each(1, pieces, first_copy, "start")

    def other_leaf(k):
        item_copy(k).wait_recv()
        their = wrap(leaf + leafs - k, leafs)
        owner, local = locate(ids[their], SUB_ITEMS, per_i)
        mark = owner == me
        rank = rank_of(ones_where(mark)).astype(I32)
        rows[their] = chosen_items(jnp.where(mark, rank, -1), local)

    def their_rows(k):
        back = leafs - k
        return back * tensors, (back + 1) * tensors

    if leafs == 2:
        other_leaf(1)
        each(tensors, 2 * tensors, rows_copy(0), "start")
    else:

        @pl.loop(1, leafs)
        def _(k):
            other_leaf(k)
            first, last = their_rows(k)
            each(first, last, rows_copy(0), "start")

    for h in range(1, halves):
        each(1, owners, rows_copy(h), "start")

    place = (own_owner * cap_i + own_rank).astype(F32)
    place = jnp.transpose(place).astype(I32)
    slots_n = owners * cap_i
    for u in range(users):
        hot[u] = ones_where(place[:, u : u + 1] == iota((items, slots_n), 1))
    lk[0:width, 0:cols] = proj[two:, :]
    lk[width + 2 * users :, :] = jnp.zeros((width - 2 * users, 3 * cols), BF16)

    each(1, tensors, part_copy, "wait_recv")
    qall[piece] = jnp.sum(ppi[...].astype(F32), axis=0).astype(BF16)

    def second_copy(k):
        return remote(qall.at[piece], qall.at[piece], q_s, q_r, k, same)

    each(1, pieces, second_copy, "start")
    each(1, tensors, q_copy, "wait_recv")
    q_user = weight
    for t in range(tensors):
        q_user = q_user + unfold(qin[t].astype(F32))

    each(1, owners, sums_copy, "wait_recv")
    interest = jnp.sum(pbuf[...], axis=0) * (1.0 / math.sqrt(owners * beams))
    interest_o[...] = interest
    near = interest.astype(BF16)
    a_user = a_user + dot(near, proj[width:two, :])
    each(1, pieces, first_copy, "wait_recv")
    both = fall[...].reshape(2 * width, cols)
    h_user = h_user + dot(near, both[:width])
    lk[0:width, cols : 2 * cols] = both[width:]
    each(1, pieces, second_copy, "wait_recv")
    both = qall[...].reshape(2 * width, cols)
    q_user = q_user + dot(near, both[:width])
    lk[0:width, 2 * cols :] = both[width:]
    lk[width : width + 2 * users, :] = split(jnp.concatenate([a_user, h_user, q_user], axis=1))

    last = weight * cb[1:2, :]
    n = upr * items
    half = min(cols, 256)
    logit = jnp.zeros((users, items), F32)
    for g in range(groups):
        if g % (groups // halves) == 0:
            each(1, owners, rows_copy(g // (groups // halves)), "wait_recv")
        got = arr[:, g * cap_i : (g + 1) * cap_i, :].reshape(slots_n, width)
        vec = dot(hot[g * upr : (g + 1) * upr].reshape(n, slots_n), got).astype(BF16)
        who = g * upr + iota((n, width), 0) // items
        z = jnp.concatenate([vec, ones_where((who == user_lane) & pair_lane)], axis=1)
        total = jnp.zeros((n, LANES), F32)
        for at in range(0, cols, half):
            x0 = dot(z, lk[:, at : at + half])
            mixed = dot(z, lk[:, cols + at : cols + at + half])
            second = dot(z, lk[:, 2 * cols + at : 2 * cols + at + half])
            term = x0 * (mixed * second + last[:, at : at + half])
            for j in range(0, half, LANES):
                total = total + term[:, j : j + LANES]
        high = total.astype(BF16)
        low = (total - high.astype(F32)).astype(BF16)
        for u in range(upr):
            line = ones_where(iota((users, LANES), 0) == g * upr + u)
            held = slice(u * items, (u + 1) * items)
            logit = logit + dot_nt(line, high[held]) + dot_nt(line, low[held])
    lbuf[tensor] = logit

    def logit_copy(k):
        return remote(lbuf.at[tensor], lbuf.at[tensor], l_s, l_r, k, along)

    each(1, tensors, logit_copy, "start")

    each(1, owners, score_copy, "wait_recv")
    flat = jnp.sum(sin[...], axis=0)
    flat = jnp.broadcast_to(flat, (users, spots))
    by_user = flat
    for u in range(1, users):
        turned = pltpu.roll(flat, spots - u * beams, axis=1)
        by_user = jnp.where(iota((users, spots), 0) == u, turned, by_user)
    score_o[...] = by_user[:, :beams]

    each(1, owners, beam_copy, "wait_send")
    each(1, leafs, item_copy, "wait_send")
    each(1, tensors, proj_copy, "wait_send")
    for h in range(halves):
        each(1, owners, rows_copy(h), "wait_send")
    each(1, owners, sums_copy, "wait_send")
    each(1, owners, score_copy, "wait_send")
    each(1, tensors, part_copy, "wait_send")
    each(1, pieces, first_copy, "wait_send")
    each(1, tensors, a_copy, "wait_send")
    each(1, tensors, q_copy, "wait_send")
    each(1, pieces, second_copy, "wait_send")
    each(1, tensors, logit_copy, "wait")
    logit_o[...] = jnp.sum(lbuf[...], axis=0)


def hand_over(*refs):
    n = len(refs) // 2
    copies = [pltpu.make_async_copy(refs[i], refs[n + i], refs[2 * n].at[i]) for i in range(n)]
    for copy in copies:
        copy.start()
    for copy in copies:
        copy.wait()


def per_device(*args):
    (user_feat, beam_nodes, item_ids, subtree_slot, node_table, item_table, mlp_user, mlp_node, mlp_bias, mlp_out,
     proj_in, cross_w, cross_b, out_w) = args
    leafs, tensors, user_count = (lax.axis_size(a) for a in ("leaf", "tensor", "user"))
    owners = leafs * tensors
    users, beams = beam_nodes.shape
    items = item_ids.shape[1]
    width = user_feat.shape[1]
    hidden_n = mlp_user.shape[1]
    cols = proj_in.shape[1]
    spots = users * beams
    cap_b = -(-max(2, -(-spots // owners)) // 8) * 8
    fetch = users * items // tensors
    cap_run = max(2, -(-fetch // owners))
    upr = next(
        u for u in range(1, users + 1)
        if users % u == 0 and u * items % fetch == 0 and (u * items // fetch * cap_run % 16 == 0 or u == users)
    )
    cap_i = upr * items // fetch * cap_run
    groups = users // upr
    split_leaf = 2 * width % (leafs * user_count * 16) == 0
    pieces = user_count * (leafs if split_leaf else 1)
    prow = 2 * width // pieces
    cfg = (
        leafs, tensors, user_count, upr, cap_i, cap_b,
        node_table.shape[0] // SUB_NODES, item_table.shape[0] // SUB_ITEMS, split_leaf,
    )
    vmem = pltpu.VMEM
    dma = pltpu.SemaphoreType.DMA
    scratch = [
        vmem(user_feat.shape, BF16),
        vmem(beam_nodes.shape, I32),
        vmem((leafs, users, items), I32),
        pltpu.SMEM(subtree_slot.shape, I32),
        vmem(node_table.shape, BF16),
        vmem(item_table.shape, BF16),
        vmem(mlp_user.shape, BF16),
        vmem((2 * width, hidden_n), BF16),
        vmem(mlp_bias.shape, F32),
        vmem(mlp_out.shape, BF16),
        vmem(proj_in.shape, BF16),
        vmem(cross_w.shape, BF16),
        vmem(cross_b.shape, F32),
        vmem(out_w.shape, BF16),
        dma((15,)),
        vmem((owners, 1, spots), I32),
        vmem((leafs, groups * cap_i, width), BF16),
        vmem((owners, groups * cap_i, width), BF16),
        vmem((owners, users, width), F32),
        vmem((owners, 1, spots), F32),
        vmem((owners, 1, spots), F32),
        vmem((tensors, 2 * users, cols // 2), BF16),
        vmem((tensors, 2 * users, cols // 2), BF16),
        vmem((tensors, 2 * users, cols // 2), BF16),
        vmem((tensors, prow, cols), BF16),
        vmem((pieces, prow, cols), BF16),
        vmem((tensors, prow, cols), BF16),
        vmem((tensors, prow, cols), BF16),
        vmem((pieces, prow, cols), BF16),
        vmem((2 * width, 3 * cols), BF16),
        vmem((users, items, owners * cap_i), BF16),
        vmem((tensors, users, items), F32),
    ]
    for n in (owners, leafs, tensors):
        scratch += [dma((n - 1,))] * 2
    scratch += [dma((2, owners - 1))] * 2
    for n in (owners, owners, tensors, tensors, pieces, tensors, pieces, tensors):
        scratch += [dma((n - 1,))] * 2
    spec = pl.BlockSpec(memory_space=pltpu.VMEM)
    results = (
        jax.ShapeDtypeStruct((users, beams), F32),
        jax.ShapeDtypeStruct((users, width), F32),
        jax.ShapeDtypeStruct((users, items), F32),
    )
    found = pl.pallas_call(
        functools.partial(kernel, cfg),
        out_shape=results,
        in_specs=[pl.BlockSpec(memory_space=pl.ANY)] * len(args),
        out_specs=(spec, spec, spec),
        scratch_shapes=scratch,
        compiler_params=pltpu.CompilerParams(
            collective_id=0, has_side_effects=True, vmem_limit_bytes=56 << 20
        ),
    )(*args)
    return pl.pallas_call(
        hand_over, out_shape=results,
        in_specs=[pl.BlockSpec(memory_space=pl.ANY)] * 3,
        out_specs=(pl.BlockSpec(memory_space=pl.ANY),) * 3,
        scratch_shapes=[pltpu.SemaphoreType.DMA((3,))],
        compiler_params=pltpu.CompilerParams(vmem_limit_bytes=56 << 20),
    )(*found)


def solution(mesh):
    placed = (
        P("user", None),
        P("user", BOTH),
        P("user", "leaf"),
        P(),
        P(BOTH, None),
        P(BOTH, None),
        P(),
        P(),
        P(),
        P(),
        P(None, "tensor"),
        P(None, None, "tensor"),
        P(None, "tensor"),
        P("tensor"),
    )
    return jax.shard_map(
        per_device,
        mesh=mesh,
        in_specs=placed,
        out_specs=(P("user", BOTH), P("user", None), P("user", "leaf")),
        check_vma=False,
    )
```

```python
import functools
import math

import jax
import jax.numpy as jnp
from jax import lax
from jax.experimental import pallas as pl
from jax.experimental.pallas import tpu as pltpu
from jax.sharding import PartitionSpec as P

SUB_NODES = 512
SUB_ITEMS = 512
BOTH = ("leaf", "tensor")
F32 = jnp.float32
BF16 = jnp.bfloat16
I32 = jnp.int32
LANES = 128


def dot(left, right):
    return jnp.dot(left, right, preferred_element_type=F32)


def dot_nt(left, right):
    return lax.dot_general(left, right, (((1,), (1,)), ((), ())), preferred_element_type=F32)


def split(x):
    high = x.astype(BF16)
    return jnp.concatenate([high, (x - high.astype(F32)).astype(BF16)], axis=0)


def iota(shape, axis):
    return lax.broadcasted_iota(I32, shape, axis)


def ones_where(mask):
    return jnp.where(mask, 1.0, 0.0).astype(BF16)


def log2(n):
    assert n & (n - 1) == 0
    return n.bit_length() - 1


def kernel(
    cfg, uf_h, beam_h, item_h, slot_h, node_h, itab_h, mu_h, mn_h, mb_h, mo_h, proj_h, cw_h, cb_h, ow_h,
    score_o, interest_o, logit_o,
    uf, beam, ids, slots, node, itab, mu, mlp, mb, mo, proj, cw, cb, ow, in_sem,
    brow, rows, arr, pbuf, sout, sin, abuf, qout, qin, pall, fall, ppo, ppi, qall, lk, hot, lbuf,
    b_s, b_r, i_s, i_r, p_s, p_r, r_s, r_r, n_s, n_r, c_s, c_r, a_s, a_r, u_s, u_r, f_s, f_r, w_s, w_r, q_s, q_r, l_s, l_r,
):
    leafs, tensors, user_count, upr, cap_i, cap_b, per_n, per_i, split_leaf = cfg
    leaf, tensor, user = (lax.axis_index(a) for a in ("leaf", "tensor", "user"))
    owners = leafs * tensors
    me = leaf * tensors + tensor
    users, items = ids.shape[1:]
    width = uf.shape[1]
    two = 2 * width
    cols = proj.shape[1]
    beams = beam.shape[1]
    spots = users * beams
    groups = users // upr
    hidden_n = mu.shape[1]
    pleafs = leafs if split_leaf else 1
    pieces = pleafs * user_count
    piece = user * pleafs + (leaf if split_leaf else 0)
    prow = 2 * width // pieces

    def wrap(at, n):
        return at & (n - 1) if n & (n - 1) == 0 else at % n

    def wide(k):
        kl, kt = k // tensors, k % tensors
        return {"leaf": wrap(leaf + kl, leafs), "tensor": wrap(tensor + kt, tensors)}

    def along(k):
        return {"tensor": wrap(tensor + k, tensors)}

    def across(k):
        return {"leaf": wrap(leaf + k, leafs)}

    def same(k):
        if not split_leaf:
            return {"user": wrap(user + k, user_count)}
        ku, kl = k // pleafs, k % pleafs
        return {"user": wrap(user + ku, user_count), "leaf": wrap(leaf + kl, leafs)}

    def remote(src, dst, ssem, rsem, k, who):
        return pltpu.make_async_remote_copy(
            src_ref=src, dst_ref=dst, send_sem=ssem.at[k - 1], recv_sem=rsem.at[k - 1],
            device_id=who(k), device_id_type=pl.DeviceIdType.MESH,
        )

    def loop(first, last, one):
        if isinstance(first, int) and last - first <= 8:
            for k in range(first, last):
                one(k)
        else:
            pl.loop(first, last)(one)

    def each(first, last, make, what):
        loop(first, last, lambda k: getattr(make(k), what)())

    loads = {}

    def load(name, src, dst):
        loads[name] = pltpu.make_async_copy(src, dst, in_sem.at[len(loads)])
        loads[name].start()

    load("slots", slot_h, slots)
    load("beam", beam_h, beam)
    load("ids", item_h, ids.at[leaf])
    load("proj", proj_h, proj)
    load("uf", uf_h, uf)
    load("itab", itab_h, itab)
    load("mu", mu_h, mu)
    load("mn", mn_h, mlp.at[pl.ds(0, width)])
    load("mb", mb_h, mb)
    load("mo", mo_h, mo)
    load("node", node_h, node)
    load("ow", ow_h, ow)
    load("w1", cw_h.at[1], cw.at[1])
    load("cb", cb_h, cb)
    load("w0", cw_h.at[0], cw.at[0])

    def fold(x):
        return jnp.concatenate([x[:, : cols // 2], x[:, cols // 2 :]], axis=0).astype(BF16)

    def unfold(x):
        return jnp.concatenate([x[:users], x[users:]], axis=1)

    barrier = pltpu.get_barrier_semaphore()

    def greet(who):
        def one(k):
            pl.semaphore_signal(barrier, inc=1, device_id=who(k), device_id_type=pl.DeviceIdType.MESH)
        return one

    loop(1, owners, greet(wide))
    loop(pleafs, pieces, greet(same))

    loads["beam"].wait()
    spread = jnp.concatenate([beam[...], jnp.zeros((users, spots - beams), I32)], axis=1)
    spread = pltpu.roll(spread, 0, axis=1, stride=beams, stride_axis=0)
    mine = iota((users, spots), 1) // beams == iota((users, spots), 0)
    brow[me] = jnp.sum(jnp.where(mine, spread, 0), axis=0, keepdims=True)
    loads["ids"].wait()
    loads["proj"].wait()
    pall[tensor] = proj[pl.ds(pl.multiple_of(width + piece * prow, prow), prow), :]
    loads["uf"].wait()
    a_user = dot(uf[...], proj[:width, :])
    abuf[tensor] = fold(a_user)

    pl.semaphore_wait(barrier, owners - 1 + pieces - pleafs)

    def item_copy(k):
        return remote(ids.at[leaf], ids.at[leaf], i_s, i_r, k, across)

    def beam_copy(k):
        return remote(brow.at[me], brow.at[me], b_s, b_r, k, wide)

    def proj_copy(k):
        return remote(pall.at[tensor], pall.at[tensor], p_s, p_r, k, along)

    def a_copy(k):
        return remote(abuf.at[tensor], abuf.at[tensor], a_s, a_r, k, along)

    each(1, owners, beam_copy, "start")
    each(1, leafs, item_copy, "start")
    each(1, tensors, proj_copy, "start")
    each(1, tensors, a_copy, "start")

    loads["slots"].wait()
    n_sub = slots.shape[0]

    def locate(at, span, per):
        sub = at >> log2(span)

        def one(s, slot):
            return jnp.where(sub == s, slots[s], slot)

        slot = lax.fori_loop(0, n_sub, one, jnp.zeros_like(at), unroll=min(n_sub, 32))
        return slot >> log2(per), ((slot & (per - 1)) << log2(span)) + (at & (span - 1))

    before = ones_where(iota((items, items), 0) < iota((items, items), 1))
    alls = jnp.ones((items, items), BF16)

    def rank_of(marks):
        n = marks.shape[0]
        r, c = iota((n, n), 0), iota((n, n), 1)
        earlier = ones_where((r // upr == c // upr) & (c < r))
        return dot(marks, before) + dot(earlier, dot(marks, alls).astype(BF16))

    def pick(table, wanted):
        n, total = wanted.shape[0], table.shape[0]
        step = min(total, 512)
        out = jnp.zeros((n, width), F32)
        for at in range(0, total, step):
            hit = ones_where(wanted - at == iota((n, step), 1))
            out = out + dot(hit, table[at : at + step, :])
        return out.astype(BF16)

    def chosen_items(rank, local):
        s = iota((cap_i, items), 0)
        lists = []
        for g in range(groups):
            total = jnp.zeros((cap_i, items), I32)
            for u in range(g * upr, (g + 1) * upr):
                total = total + jnp.where(rank[u : u + 1, :] == s, local[u : u + 1, :] + 1, 0)
            lists.append(jnp.sum(total, axis=1, keepdims=True) - 1)
        return pick(itab, jnp.concatenate(lists, axis=0))

    loads["ow"].wait()
    loads["w1"].wait()
    weight = ow[...].astype(F32).reshape(1, cols)
    left = jnp.concatenate([pall[tensor].astype(F32), a_user], axis=0) * weight
    part = dot_nt(left.astype(BF16), cw[1])
    for t in range(tensors):
        held = part[:, t * cols : (t + 1) * cols]
        ppo[t] = held[:prow].astype(BF16)
        qout[t] = fold(held[prow:])
    ppi[tensor] = ppo[tensor]
    qin[tensor] = qout[tensor]

    def part_copy(k):
        return remote(ppo.at[wrap(tensor + k, tensors)], ppi.at[tensor], w_s, w_r, k, along)

    def q_copy(k):
        return remote(qout.at[wrap(tensor + k, tensors)], qin.at[tensor], u_s, u_r, k, along)

    each(1, tensors, part_copy, "start")
    each(1, tensors, q_copy, "start")

    own_owner, own_local = locate(ids[leaf], SUB_ITEMS, per_i)
    marks3 = own_owner[None] == iota((owners, users, items), 0)
    ranks3 = rank_of(ones_where(marks3).reshape(owners * users, items)).reshape(owners, users, items)
    own_rank = jnp.sum(jnp.where(marks3, ranks3, 0.0), axis=0).astype(I32)
    loads["itab"].wait()
    picked = chosen_items(jnp.where(own_owner == me, own_rank, -1), own_local)
    rows[leaf] = picked
    arr[me] = picked

    halves = groups
    held_rows = groups * cap_i // halves

    def rows_copy(h):
        part = pl.ds(h * held_rows, held_rows)

        def one(k):
            return remote(
                rows.at[wrap(leaf + k // tensors, leafs), part], arr.at[me, part],
                r_s.at[h], r_r.at[h], k, wide,
            )
        return one

    each(1, tensors, rows_copy(0), "start")

    for name in ("mu", "mb", "mn", "mo"):
        loads[name].wait()
    up = dot(uf[...], mu[...]) + mb[...].reshape(1, hidden_n)
    mlp[width : width + 2 * users, :] = split(up)
    mlp[width + 2 * users :, :] = jnp.zeros((width - 2 * users, hidden_n), BF16)
    shared_lane = iota((1, width), 1)
    pair_lane = shared_lane < 2 * users
    user_lane = shared_lane & (users - 1)

    each(1, owners, beam_copy, "wait_recv")
    n_owner, n_local = locate(brow[:, 0, :], SUB_NODES, per_n)
    n_mark = n_owner == me
    n_rank = dot(ones_where(n_mark), ones_where(iota((spots, spots), 0) < iota((spots, spots), 1)))
    n_rank = jnp.where(n_mark, n_rank.astype(I32), -1)
    coded = n_local * users + iota((owners, spots), 1) // beams + 1
    n_hit = n_rank[:, None, :] == iota((owners, cap_b, spots), 1)
    places = owners * cap_b
    code = jnp.sum(jnp.where(n_hit, coded[:, None, :], 0), axis=2, keepdims=True).reshape(places, 1) - 1
    loads["node"].wait()
    node_rows = pick(node, code >> log2(users))
    user_hot = (code >= 0) & ((code & (users - 1)) == user_lane) & pair_lane
    left = jnp.concatenate([node_rows, ones_where(user_hot)], axis=1)
    step = min(hidden_n, 256)
    score = jnp.zeros((users, places), F32)
    out_row = jnp.broadcast_to(mo[...].reshape(1, hidden_n), (users, hidden_n))
    for at in range(0, hidden_n, step):
        half = 0.5 * dot(left, mlp[:, at : at + step])
        hidden = (half + half * jnp.tanh(half)).astype(BF16)
        score = score + dot_nt(out_row[:, at : at + step], hidden)
    gate = 0.5 + 0.5 * jnp.tanh(0.5 * score)
    gate = gate * jnp.transpose(jnp.where(user_hot, 1.0, 0.0))[:users, :]
    sums = dot(split(gate), node_rows)
    pbuf[me] = sums[:users] + sums[users:]

    def sums_copy(k):
        return remote(pbuf.at[me], pbuf.at[me], n_s, n_r, k, wide)

    each(1, owners, sums_copy, "start")

    own_lane = iota((owners, places), 1) // cap_b == iota((owners, places), 0)
    score_rows = jnp.where(own_lane, score[0:1, :], 0.0)
    back = dot(split(score_rows), ones_where(n_hit.reshape(places, spots)))
    sout[...] = (back[:owners] + back[owners:])[:, None, :]
    sin[me] = sout[me]

    def score_copy(k):
        to = wide(k)
        return remote(sout.at[to["leaf"] * tensors + to["tensor"]], sin.at[me], c_s, c_r, k, wide)

    each(1, owners, score_copy, "start")

    loads["w0"].wait()
    loads["cb"].wait()
    each(1, tensors, proj_copy, "wait_recv")
    each(1, tensors, a_copy, "wait_recv")
    total = jnp.zeros((prow + users, cols), F32)
    for t in range(tensors):
        left = jnp.concatenate([pall[t], unfold(abuf[t])], axis=0)
        total = total + dot(left, cw[0, t * cols : (t + 1) * cols, :])
    fall[piece] = total[:prow].astype(BF16)
    h_user = total[prow:] + cb[0:1, :] + 1.0

    def first_copy(k):
        return remote(fall.at[piece], fall.at[piece], f_s, f_r, k, same)

    each(1, pieces, first_copy, "start")

    def other_leaf(k):
        item_copy(k).wait_recv()
        their = wrap(leaf + leafs - k, leafs)
        owner, local = locate(ids[their], SUB_ITEMS, per_i)
        mark = owner == me
        rank = rank_of(ones_where(mark)).astype(I32)
        rows[their] = chosen_items(jnp.where(mark, rank, -1), local)

    def their_rows(k):
        back = leafs - k
        return back * tensors, (back + 1) * tensors

    if leafs == 2:
        other_leaf(1)
        each(tensors, 2 * tensors, rows_copy(0), "start")
    else:

        @pl.loop(1, leafs)
        def _(k):
            other_leaf(k)
            first, last = their_rows(k)
            each(first, last, rows_copy(0), "start")

    for h in range(1, halves):
        each(1, owners, rows_copy(h), "start")

    place = (own_owner * cap_i + own_rank).astype(F32)
    place = jnp.transpose(place).astype(I32)
    slots_n = owners * cap_i
    for u in range(users):
        hot[u] = ones_where(place[:, u : u + 1] == iota((items, slots_n), 1))
    lk[0:width, 0:cols] = proj[two:, :]
    lk[width + 2 * users :, :] = jnp.zeros((width - 2 * users, 3 * cols), BF16)

    each(1, tensors, part_copy, "wait_recv")
    qall[piece] = jnp.sum(ppi[...].astype(F32), axis=0).astype(BF16)

    def second_copy(k):
        return remote(qall.at[piece], qall.at[piece], q_s, q_r, k, same)

    each(1, pieces, second_copy, "start")
    each(1, tensors, q_copy, "wait_recv")
    q_user = weight
    for t in range(tensors):
        q_user = q_user + unfold(qin[t].astype(F32))

    each(1, owners, sums_copy, "wait_recv")
    interest = jnp.sum(pbuf[...], axis=0) * (1.0 / math.sqrt(owners * beams))
    interest_o[...] = interest
    near = interest.astype(BF16)
    a_user = a_user + dot(near, proj[width:two, :])
    each(1, pieces, first_copy, "wait_recv")
    both = fall[...].reshape(2 * width, cols)
    h_user = h_user + dot(near, both[:width])
    lk[0:width, cols : 2 * cols] = both[width:]
    each(1, pieces, second_copy, "wait_recv")
    both = qall[...].reshape(2 * width, cols)
    q_user = q_user + dot(near, both[:width])
    lk[0:width, 2 * cols :] = both[width:]
    lk[width : width + 2 * users, :] = split(jnp.concatenate([a_user, h_user, q_user], axis=1))

    last = weight * cb[1:2, :]
    n = upr * items
    half = min(cols, 256)
    logit = jnp.zeros((users, items), F32)
    for g in range(groups):
        if g % (groups // halves) == 0:
            each(1, owners, rows_copy(g // (groups // halves)), "wait_recv")
        got = arr[:, g * cap_i : (g + 1) * cap_i, :].reshape(slots_n, width)
        vec = dot(hot[g * upr : (g + 1) * upr].reshape(n, slots_n), got).astype(BF16)
        who = g * upr + iota((n, width), 0) // items
        z = jnp.concatenate([vec, ones_where((who == user_lane) & pair_lane)], axis=1)
        total = jnp.zeros((n, LANES), F32)
        for at in range(0, cols, half):
            x0 = dot(z, lk[:, at : at + half])
            mixed = dot(z, lk[:, cols + at : cols + at + half])
            second = dot(z, lk[:, 2 * cols + at : 2 * cols + at + half])
            term = x0 * (mixed * second + last[:, at : at + half])
            for j in range(0, half, LANES):
                total = total + term[:, j : j + LANES]
        high = total.astype(BF16)
        low = (total - high.astype(F32)).astype(BF16)
        pair = jnp.concatenate([high, low], axis=1)
        for u in range(upr):
            line = ones_where(iota((users, 2 * LANES), 0) == g * upr + u)
            logit = logit + dot_nt(line, pair[u * items : (u + 1) * items])
    lbuf[tensor] = logit

    def logit_copy(k):
        return remote(lbuf.at[tensor], lbuf.at[tensor], l_s, l_r, k, along)

    each(1, tensors, logit_copy, "start")

    each(1, owners, score_copy, "wait_recv")
    flat = jnp.sum(sin[...], axis=0)
    flat = jnp.broadcast_to(flat, (users, spots))
    by_user = flat
    for u in range(1, users):
        turned = pltpu.roll(flat, spots - u * beams, axis=1)
        by_user = jnp.where(iota((users, spots), 0) == u, turned, by_user)
    score_o[...] = by_user[:, :beams]

    each(1, owners, beam_copy, "wait_send")
    each(1, leafs, item_copy, "wait_send")
    each(1, tensors, proj_copy, "wait_send")
    for h in range(halves):
        each(1, owners, rows_copy(h), "wait_send")
    each(1, owners, sums_copy, "wait_send")
    each(1, owners, score_copy, "wait_send")
    each(1, tensors, part_copy, "wait_send")
    each(1, pieces, first_copy, "wait_send")
    each(1, tensors, a_copy, "wait_send")
    each(1, tensors, q_copy, "wait_send")
    each(1, pieces, second_copy, "wait_send")
    each(1, tensors, logit_copy, "wait")
    logit_o[...] = jnp.sum(lbuf[...], axis=0)


def hand_over(*refs):
    n = len(refs) // 2
    for src, out in zip(refs[:n], refs[n:]):
        out[...] = src[...]


def per_device(*args):
    (user_feat, beam_nodes, item_ids, subtree_slot, node_table, item_table, mlp_user, mlp_node, mlp_bias, mlp_out,
     proj_in, cross_w, cross_b, out_w) = args
    leafs, tensors, user_count = (lax.axis_size(a) for a in ("leaf", "tensor", "user"))
    owners = leafs * tensors
    users, beams = beam_nodes.shape
    items = item_ids.shape[1]
    width = user_feat.shape[1]
    hidden_n = mlp_user.shape[1]
    cols = proj_in.shape[1]
    spots = users * beams
    cap_b = -(-max(2, -(-spots // owners)) // 8) * 8
    fetch = users * items // tensors
    cap_run = max(2, -(-fetch // owners))
    upr = next(
        u for u in range(1, users + 1)
        if users % u == 0 and u * items % fetch == 0 and (u * items // fetch * cap_run % 16 == 0 or u == users)
    )
    cap_i = upr * items // fetch * cap_run
    groups = users // upr
    split_leaf = 2 * width % (leafs * user_count * 16) == 0
    pieces = user_count * (leafs if split_leaf else 1)
    prow = 2 * width // pieces
    cfg = (
        leafs, tensors, user_count, upr, cap_i, cap_b,
        node_table.shape[0] // SUB_NODES, item_table.shape[0] // SUB_ITEMS, split_leaf,
    )
    vmem = pltpu.VMEM
    dma = pltpu.SemaphoreType.DMA
    scratch = [
        vmem(user_feat.shape, BF16),
        vmem(beam_nodes.shape, I32),
        vmem((leafs, users, items), I32),
        pltpu.SMEM(subtree_slot.shape, I32),
        vmem(node_table.shape, BF16),
        vmem(item_table.shape, BF16),
        vmem(mlp_user.shape, BF16),
        vmem((2 * width, hidden_n), BF16),
        vmem(mlp_bias.shape, F32),
        vmem(mlp_out.shape, BF16),
        vmem(proj_in.shape, BF16),
        vmem(cross_w.shape, BF16),
        vmem(cross_b.shape, F32),
        vmem(out_w.shape, BF16),
        dma((15,)),
        vmem((owners, 1, spots), I32),
        vmem((leafs, groups * cap_i, width), BF16),
        vmem((owners, groups * cap_i, width), BF16),
        vmem((owners, users, width), F32),
        vmem((owners, 1, spots), F32),
        vmem((owners, 1, spots), F32),
        vmem((tensors, 2 * users, cols // 2), BF16),
        vmem((tensors, 2 * users, cols // 2), BF16),
        vmem((tensors, 2 * users, cols // 2), BF16),
        vmem((tensors, prow, cols), BF16),
        vmem((pieces, prow, cols), BF16),
        vmem((tensors, prow, cols), BF16),
        vmem((tensors, prow, cols), BF16),
        vmem((pieces, prow, cols), BF16),
        vmem((2 * width, 3 * cols), BF16),
        vmem((users, items, owners * cap_i), BF16),
        vmem((tensors, users, items), F32),
    ]
    for n in (owners, leafs, tensors):
        scratch += [dma((n - 1,))] * 2
    scratch += [dma((groups, owners - 1))] * 2
    for n in (owners, owners, tensors, tensors, pieces, tensors, pieces, tensors):
        scratch += [dma((n - 1,))] * 2
    spec = pl.BlockSpec(memory_space=pltpu.VMEM)
    results = (
        jax.ShapeDtypeStruct((users, beams), F32),
        jax.ShapeDtypeStruct((users, width), F32),
        jax.ShapeDtypeStruct((users, items), F32),
    )
    found = pl.pallas_call(
        functools.partial(kernel, cfg),
        out_shape=results,
        in_specs=[pl.BlockSpec(memory_space=pl.ANY)] * len(args),
        out_specs=(spec, spec, spec),
        scratch_shapes=scratch,
        compiler_params=pltpu.CompilerParams(
            collective_id=0, has_side_effects=True, vmem_limit_bytes=56 << 20
        ),
    )(*args)
    return pl.pallas_call(
        hand_over, out_shape=results,
        in_specs=[spec] * 3,
        out_specs=(spec,) * 3,
        compiler_params=pltpu.CompilerParams(vmem_limit_bytes=56 << 20),
    )(*found)


def solution(mesh):
    placed = (
        P("user", None),
        P("user", BOTH),
        P("user", "leaf"),
        P(),
        P(BOTH, None),
        P(BOTH, None),
        P(),
        P(),
        P(),
        P(),
        P(None, "tensor"),
        P(None, None, "tensor"),
        P(None, "tensor"),
        P("tensor"),
    )
    return jax.shard_map(
        per_device,
        mesh=mesh,
        in_specs=placed,
        out_specs=(P("user", BOTH), P("user", None), P("user", "leaf")),
        check_vma=False,
    )
```

```python
import functools
import math

import jax
import jax.numpy as jnp
from jax import lax
from jax.experimental import pallas as pl
from jax.experimental.pallas import tpu as pltpu
from jax.sharding import PartitionSpec as P

SUB_NODES = 512
SUB_ITEMS = 512
BOTH = ("leaf", "tensor")
F32 = jnp.float32
BF16 = jnp.bfloat16
I32 = jnp.int32
LANES = 128


def dot(left, right):
    return jnp.dot(left, right, preferred_element_type=F32)


def dot_nt(left, right):
    return lax.dot_general(left, right, (((1,), (1,)), ((), ())), preferred_element_type=F32)


def split(x):
    high = x.astype(BF16)
    return jnp.concatenate([high, (x - high.astype(F32)).astype(BF16)], axis=0)


def iota(shape, axis):
    return lax.broadcasted_iota(I32, shape, axis)


def ones_where(mask):
    return jnp.where(mask, 1.0, 0.0).astype(BF16)


def log2(n):
    assert n & (n - 1) == 0
    return n.bit_length() - 1


def kernel(
    cfg, uf_h, beam_h, item_h, slot_h, node_h, itab_h, mu_h, mn_h, mb_h, mo_h, proj_h, cw_h, cb_h, ow_h,
    score_o, interest_o, logit_o,
    uf, beam, ids, slots, node, itab, mu, mlp, mb, mo, proj, cw, cb, ow, in_sem,
    brow, rows, arr, pbuf, sout, sin, abuf, qout, qin, pall, fall, ppo, ppi, qall, lk, hot, lbuf,
    b_s, b_r, i_s, i_r, p_s, p_r, r_s, r_r, n_s, n_r, c_s, c_r, a_s, a_r, u_s, u_r, f_s, f_r, w_s, w_r, q_s, q_r, l_s, l_r,
):
    leafs, tensors, user_count, upr, cap_i, cap_b, per_n, per_i, split_leaf = cfg
    leaf, tensor, user = (lax.axis_index(a) for a in ("leaf", "tensor", "user"))
    owners = leafs * tensors
    me = leaf * tensors + tensor
    users, items = ids.shape[1:]
    width = uf.shape[1]
    two = 2 * width
    cols = proj.shape[1]
    beams = beam.shape[1]
    spots = users * beams
    groups = users // upr
    hidden_n = mu.shape[1]
    pleafs = leafs if split_leaf else 1
    pieces = pleafs * user_count
    piece = user * pleafs + (leaf if split_leaf else 0)
    prow = 2 * width // pieces

    def partner(at, k, n):
        assert n & (n - 1) == 0
        return at + k - 2 * (at & k)

    def wide(k):
        kl, kt = k // tensors, k % tensors
        return {"leaf": partner(leaf, kl, leafs), "tensor": partner(tensor, kt, tensors)}

    def along(k):
        return {"tensor": partner(tensor, k, tensors)}

    def across(k):
        return {"leaf": partner(leaf, k, leafs)}

    def same(k):
        if not split_leaf:
            return {"user": partner(user, k, user_count)}
        ku, kl = k // pleafs, k % pleafs
        return {"user": partner(user, ku, user_count), "leaf": partner(leaf, kl, leafs)}

    def remote(src, dst, ssem, rsem, k, who):
        return pltpu.make_async_remote_copy(
            src_ref=src, dst_ref=dst, send_sem=ssem.at[k - 1], recv_sem=rsem.at[k - 1],
            device_id=who(k), device_id_type=pl.DeviceIdType.MESH,
        )

    def loop(first, last, one):
        if isinstance(first, int) and last - first <= 8:
            for k in range(first, last):
                one(k)
        else:
            pl.loop(first, last)(one)

    def each(first, last, make, what):
        loop(first, last, lambda k: getattr(make(k), what)())

    loads = {}

    def load(name, src, dst):
        loads[name] = pltpu.make_async_copy(src, dst, in_sem.at[len(loads)])
        loads[name].start()

    load("slots", slot_h, slots)
    load("beam", beam_h, beam)
    load("ids", item_h, ids.at[leaf])
    load("proj", proj_h, proj)
    load("uf", uf_h, uf)
    load("itab", itab_h, itab)
    load("mu", mu_h, mu)
    load("mn", mn_h, mlp.at[pl.ds(0, width)])
    load("mb", mb_h, mb)
    load("mo", mo_h, mo)
    load("node", node_h, node)
    load("ow", ow_h, ow)
    load("w1", cw_h.at[1], cw.at[1])
    load("cb", cb_h, cb)
    load("w0", cw_h.at[0], cw.at[0])

    def fold(x):
        return jnp.concatenate([x[:, : cols // 2], x[:, cols // 2 :]], axis=0).astype(BF16)

    def unfold(x):
        return jnp.concatenate([x[:users], x[users:]], axis=1)

    barrier = pltpu.get_barrier_semaphore()

    def greet(who):
        def one(k):
            pl.semaphore_signal(barrier, inc=1, device_id=who(k), device_id_type=pl.DeviceIdType.MESH)
        return one

    loop(1, owners, greet(wide))
    loop(pleafs, pieces, greet(same))

    loads["beam"].wait()
    spread = jnp.concatenate([beam[...], jnp.zeros((users, spots - beams), I32)], axis=1)
    spread = pltpu.roll(spread, 0, axis=1, stride=beams, stride_axis=0)
    mine = iota((users, spots), 1) // beams == iota((users, spots), 0)
    brow[me] = jnp.sum(jnp.where(mine, spread, 0), axis=0, keepdims=True)
    loads["ids"].wait()
    loads["proj"].wait()
    pall[tensor] = proj[pl.ds(pl.multiple_of(width + piece * prow, prow), prow), :]
    loads["uf"].wait()
    a_user = dot(uf[...], proj[:width, :])
    abuf[tensor] = fold(a_user)

    loads["slots"].wait()
    n_sub = slots.shape[0]

    def locate(at, span, per):
        sub = at >> log2(span)

        def one(s, slot):
            return jnp.where(sub == s, slots[s], slot)

        slot = lax.fori_loop(0, n_sub, one, jnp.zeros_like(at), unroll=min(n_sub, 32))
        return slot >> log2(per), ((slot & (per - 1)) << log2(span)) + (at & (span - 1))

    before = ones_where(iota((items, items), 0) < iota((items, items), 1))
    alls = jnp.ones((items, items), BF16)

    def rank_of(marks):
        n = marks.shape[0]
        r, c = iota((n, n), 0), iota((n, n), 1)
        earlier = ones_where((r // upr == c // upr) & (c < r))
        return dot(marks, before) + dot(earlier, dot(marks, alls).astype(BF16))

    def pick(table, wanted):
        n, total = wanted.shape[0], table.shape[0]
        step = min(total, 512)
        out = jnp.zeros((n, width), F32)
        for at in range(0, total, step):
            hit = ones_where(wanted - at == iota((n, step), 1))
            out = out + dot(hit, table[at : at + step, :])
        return out.astype(BF16)

    def chosen_items(rank, local):
        s = iota((cap_i, items), 0)
        lists = []
        for g in range(groups):
            total = jnp.zeros((cap_i, items), I32)
            for u in range(g * upr, (g + 1) * upr):
                total = total + jnp.where(rank[u : u + 1, :] == s, local[u : u + 1, :] + 1, 0)
            lists.append(jnp.sum(total, axis=1, keepdims=True) - 1)
        return pick(itab, jnp.concatenate(lists, axis=0))

    own_owner, own_local = locate(ids[leaf], SUB_ITEMS, per_i)
    marks3 = own_owner[None] == iota((owners, users, items), 0)
    ranks3 = rank_of(ones_where(marks3).reshape(owners * users, items)).reshape(owners, users, items)
    own_rank = jnp.sum(jnp.where(marks3, ranks3, 0.0), axis=0).astype(I32)
    loads["itab"].wait()
    picked = chosen_items(jnp.where(own_owner == me, own_rank, -1), own_local)
    rows[leaf] = picked
    arr[me] = picked

    pl.semaphore_wait(barrier, owners - 1 + pieces - pleafs)

    def item_copy(k):
        return remote(ids.at[leaf], ids.at[leaf], i_s, i_r, k, across)

    def beam_copy(k):
        return remote(brow.at[me], brow.at[me], b_s, b_r, k, wide)

    def proj_copy(k):
        return remote(pall.at[tensor], pall.at[tensor], p_s, p_r, k, along)

    def a_copy(k):
        return remote(abuf.at[tensor], abuf.at[tensor], a_s, a_r, k, along)

    each(1, owners, beam_copy, "start")
    each(1, leafs, item_copy, "start")
    each(1, tensors, proj_copy, "start")
    each(1, tensors, a_copy, "start")


    loads["ow"].wait()
    loads["w1"].wait()
    weight = ow[...].astype(F32).reshape(1, cols)
    left = jnp.concatenate([pall[tensor].astype(F32), a_user], axis=0) * weight
    part = dot_nt(left.astype(BF16), cw[1])
    for t in range(tensors):
        held = part[:, t * cols : (t + 1) * cols]
        ppo[t] = held[:prow].astype(BF16)
        qout[t] = fold(held[prow:])
    ppi[tensor] = ppo[tensor]
    qin[tensor] = qout[tensor]

    def part_copy(k):
        return remote(ppo.at[partner(tensor, k, tensors)], ppi.at[tensor], w_s, w_r, k, along)

    def q_copy(k):
        return remote(qout.at[partner(tensor, k, tensors)], qin.at[tensor], u_s, u_r, k, along)

    each(1, tensors, part_copy, "start")
    each(1, tensors, q_copy, "start")

    halves = groups
    held_rows = groups * cap_i // halves

    def rows_copy(h):
        part = pl.ds(h * held_rows, held_rows)

        def one(k):
            return remote(
                rows.at[partner(leaf, k // tensors, leafs), part], arr.at[me, part],
                r_s.at[h], r_r.at[h], k, wide,
            )
        return one

    each(1, tensors, rows_copy(0), "start")


    for name in ("mu", "mb", "mn", "mo"):
        loads[name].wait()
    up = dot(uf[...], mu[...]) + mb[...].reshape(1, hidden_n)
    mlp[width : width + 2 * users, :] = split(up)
    mlp[width + 2 * users :, :] = jnp.zeros((width - 2 * users, hidden_n), BF16)
    shared_lane = iota((1, width), 1)
    pair_lane = shared_lane < 2 * users
    user_lane = shared_lane & (users - 1)

    each(1, owners, beam_copy, "wait_recv")
    n_owner, n_local = locate(brow[:, 0, :], SUB_NODES, per_n)
    n_mark = n_owner == me
    n_rank = dot(ones_where(n_mark), ones_where(iota((spots, spots), 0) < iota((spots, spots), 1)))
    n_rank = jnp.where(n_mark, n_rank.astype(I32), -1)
    coded = n_local * users + iota((owners, spots), 1) // beams + 1
    n_hit = n_rank[:, None, :] == iota((owners, cap_b, spots), 1)
    places = owners * cap_b
    code = jnp.sum(jnp.where(n_hit, coded[:, None, :], 0), axis=2, keepdims=True).reshape(places, 1) - 1
    loads["node"].wait()
    node_rows = pick(node, code >> log2(users))
    user_hot = (code >= 0) & ((code & (users - 1)) == user_lane) & pair_lane
    left = jnp.concatenate([node_rows, ones_where(user_hot)], axis=1)
    step = min(hidden_n, 256)
    score = jnp.zeros((users, places), F32)
    out_row = jnp.broadcast_to(mo[...].reshape(1, hidden_n), (users, hidden_n))
    for at in range(0, hidden_n, step):
        half = 0.5 * dot(left, mlp[:, at : at + step])
        hidden = (half + half * jnp.tanh(half)).astype(BF16)
        score = score + dot_nt(out_row[:, at : at + step], hidden)
    gate = 0.5 + 0.5 * jnp.tanh(0.5 * score)
    gate = gate * jnp.transpose(jnp.where(user_hot, 1.0, 0.0))[:users, :]
    sums = dot(split(gate), node_rows)
    pbuf[me] = sums[:users] + sums[users:]

    def sums_copy(k):
        return remote(pbuf.at[me], pbuf.at[me], n_s, n_r, k, wide)

    each(1, owners, sums_copy, "start")

    own_lane = iota((owners, places), 1) // cap_b == iota((owners, places), 0)
    score_rows = jnp.where(own_lane, score[0:1, :], 0.0)
    back = dot(split(score_rows), ones_where(n_hit.reshape(places, spots)))
    sout[...] = (back[:owners] + back[owners:])[:, None, :]
    sin[me] = sout[me]

    def score_copy(k):
        to = wide(k)
        return remote(sout.at[to["leaf"] * tensors + to["tensor"]], sin.at[me], c_s, c_r, k, wide)

    each(1, owners, score_copy, "start")

    loads["w0"].wait()
    loads["cb"].wait()
    each(1, tensors, proj_copy, "wait_recv")
    each(1, tensors, a_copy, "wait_recv")
    total = jnp.zeros((prow + users, cols), F32)
    for t in range(tensors):
        left = jnp.concatenate([pall[t], unfold(abuf[t])], axis=0)
        total = total + dot(left, cw[0, t * cols : (t + 1) * cols, :])
    fall[piece] = total[:prow].astype(BF16)
    h_user = total[prow:] + cb[0:1, :] + 1.0

    def first_copy(k):
        return remote(fall.at[piece], fall.at[piece], f_s, f_r, k, same)

    each(1, pieces, first_copy, "start")

    def other_leaf(k):
        item_copy(k).wait_recv()
        their = partner(leaf, k, leafs)
        owner, local = locate(ids[their], SUB_ITEMS, per_i)
        mark = owner == me
        rank = rank_of(ones_where(mark)).astype(I32)
        rows[their] = chosen_items(jnp.where(mark, rank, -1), local)

    def their_rows(k):
        return k * tensors, (k + 1) * tensors

    if leafs == 2:
        other_leaf(1)
        each(tensors, 2 * tensors, rows_copy(0), "start")
    else:

        @pl.loop(1, leafs)
        def _(k):
            other_leaf(k)
            first, last = their_rows(k)
            each(first, last, rows_copy(0), "start")

    for h in range(1, halves):
        each(1, owners, rows_copy(h), "start")

    each(1, tensors, part_copy, "wait_recv")
    qall[piece] = jnp.sum(ppi[...].astype(F32), axis=0).astype(BF16)

    def second_copy(k):
        return remote(qall.at[piece], qall.at[piece], q_s, q_r, k, same)

    each(1, pieces, second_copy, "start")
    each(1, tensors, q_copy, "wait_recv")
    q_user = weight
    for t in range(tensors):
        q_user = q_user + unfold(qin[t].astype(F32))

    place = (own_owner * cap_i + own_rank).astype(F32)
    place = jnp.transpose(place).astype(I32)
    slots_n = owners * cap_i
    for u in range(users):
        hot[u] = ones_where(place[:, u : u + 1] == iota((items, slots_n), 1))
    lk[0:width, 0:cols] = proj[two:, :]
    lk[width + 2 * users :, :] = jnp.zeros((width - 2 * users, 3 * cols), BF16)

    each(1, owners, sums_copy, "wait_recv")
    interest = jnp.sum(pbuf[...], axis=0) * (1.0 / math.sqrt(owners * beams))
    interest_o[...] = interest
    near = interest.astype(BF16)
    a_user = a_user + dot(near, proj[width:two, :])
    each(1, pieces, first_copy, "wait_recv")
    both = fall[...].reshape(2 * width, cols)
    h_user = h_user + dot(near, both[:width])
    lk[0:width, cols : 2 * cols] = both[width:]
    each(1, pieces, second_copy, "wait_recv")
    both = qall[...].reshape(2 * width, cols)
    q_user = q_user + dot(near, both[:width])
    lk[0:width, 2 * cols :] = both[width:]
    lk[width : width + 2 * users, :] = split(jnp.concatenate([a_user, h_user, q_user], axis=1))

    last = weight * cb[1:2, :]
    n = upr * items
    half = min(cols, 256)
    logit = jnp.zeros((users, items), F32)
    for g in range(groups):
        if g % (groups // halves) == 0:
            each(1, owners, rows_copy(g // (groups // halves)), "wait_recv")
        got = arr[:, g * cap_i : (g + 1) * cap_i, :].reshape(slots_n, width)
        vec = dot(hot[g * upr : (g + 1) * upr].reshape(n, slots_n), got).astype(BF16)
        who = g * upr + iota((n, width), 0) // items
        z = jnp.concatenate([vec, ones_where((who == user_lane) & pair_lane)], axis=1)
        total = jnp.zeros((n, LANES), F32)
        for at in range(0, cols, half):
            x0 = dot(z, lk[:, at : at + half])
            mixed = dot(z, lk[:, cols + at : cols + at + half])
            second = dot(z, lk[:, 2 * cols + at : 2 * cols + at + half])
            term = x0 * (mixed * second + last[:, at : at + half])
            for j in range(0, half, LANES):
                total = total + term[:, j : j + LANES]
        high = total.astype(BF16)
        low = (total - high.astype(F32)).astype(BF16)
        pair = jnp.concatenate([high, low], axis=1)
        for u in range(upr):
            line = ones_where(iota((users, 2 * LANES), 0) == g * upr + u)
            logit = logit + dot_nt(line, pair[u * items : (u + 1) * items])
    lbuf[tensor] = logit

    def logit_copy(k):
        return remote(lbuf.at[tensor], lbuf.at[tensor], l_s, l_r, k, along)

    each(1, tensors, logit_copy, "start")

    each(1, owners, score_copy, "wait_recv")
    flat = jnp.sum(sin[...], axis=0)
    flat = jnp.broadcast_to(flat, (users, spots))
    by_user = flat
    for u in range(1, users):
        turned = pltpu.roll(flat, spots - u * beams, axis=1)
        by_user = jnp.where(iota((users, spots), 0) == u, turned, by_user)
    score_o[...] = by_user[:, :beams]

    each(1, owners, beam_copy, "wait_send")
    each(1, leafs, item_copy, "wait_send")
    each(1, tensors, proj_copy, "wait_send")
    for h in range(halves):
        each(1, owners, rows_copy(h), "wait_send")
    each(1, owners, sums_copy, "wait_send")
    each(1, owners, score_copy, "wait_send")
    each(1, tensors, part_copy, "wait_send")
    each(1, pieces, first_copy, "wait_send")
    each(1, tensors, a_copy, "wait_send")
    each(1, tensors, q_copy, "wait_send")
    each(1, pieces, second_copy, "wait_send")
    each(1, tensors, logit_copy, "wait")
    logit_o[...] = jnp.sum(lbuf[...], axis=0)


def hand_over(*refs):
    n = len(refs) // 2
    for src, out in zip(refs[:n], refs[n:]):
        out[...] = src[...]


def per_device(*args):
    (user_feat, beam_nodes, item_ids, subtree_slot, node_table, item_table, mlp_user, mlp_node, mlp_bias, mlp_out,
     proj_in, cross_w, cross_b, out_w) = args
    leafs, tensors, user_count = (lax.axis_size(a) for a in ("leaf", "tensor", "user"))
    owners = leafs * tensors
    users, beams = beam_nodes.shape
    items = item_ids.shape[1]
    width = user_feat.shape[1]
    hidden_n = mlp_user.shape[1]
    cols = proj_in.shape[1]
    spots = users * beams
    cap_b = -(-max(2, -(-spots // owners)) // 8) * 8
    fetch = users * items // tensors
    cap_run = max(2, -(-fetch // owners))
    upr = next(
        u for u in range(1, users + 1)
        if users % u == 0 and u * items % fetch == 0 and (u * items // fetch * cap_run % 16 == 0 or u == users)
    )
    cap_i = upr * items // fetch * cap_run
    groups = users // upr
    split_leaf = 2 * width % (leafs * user_count * 16) == 0
    pieces = user_count * (leafs if split_leaf else 1)
    prow = 2 * width // pieces
    cfg = (
        leafs, tensors, user_count, upr, cap_i, cap_b,
        node_table.shape[0] // SUB_NODES, item_table.shape[0] // SUB_ITEMS, split_leaf,
    )
    vmem = pltpu.VMEM
    dma = pltpu.SemaphoreType.DMA
    scratch = [
        vmem(user_feat.shape, BF16),
        vmem(beam_nodes.shape, I32),
        vmem((leafs, users, items), I32),
        pltpu.SMEM(subtree_slot.shape, I32),
        vmem(node_table.shape, BF16),
        vmem(item_table.shape, BF16),
        vmem(mlp_user.shape, BF16),
        vmem((2 * width, hidden_n), BF16),
        vmem(mlp_bias.shape, F32),
        vmem(mlp_out.shape, BF16),
        vmem(proj_in.shape, BF16),
        vmem(cross_w.shape, BF16),
        vmem(cross_b.shape, F32),
        vmem(out_w.shape, BF16),
        dma((15,)),
        vmem((owners, 1, spots), I32),
        vmem((leafs, groups * cap_i, width), BF16),
        vmem((owners, groups * cap_i, width), BF16),
        vmem((owners, users, width), F32),
        vmem((owners, 1, spots), F32),
        vmem((owners, 1, spots), F32),
        vmem((tensors, 2 * users, cols // 2), BF16),
        vmem((tensors, 2 * users, cols // 2), BF16),
        vmem((tensors, 2 * users, cols // 2), BF16),
        vmem((tensors, prow, cols), BF16),
        vmem((pieces, prow, cols), BF16),
        vmem((tensors, prow, cols), BF16),
        vmem((tensors, prow, cols), BF16),
        vmem((pieces, prow, cols), BF16),
        vmem((2 * width, 3 * cols), BF16),
        vmem((users, items, owners * cap_i), BF16),
        vmem((tensors, users, items), F32),
    ]
    for n in (owners, leafs, tensors):
        scratch += [dma((n - 1,))] * 2
    scratch += [dma((groups, owners - 1))] * 2
    for n in (owners, owners, tensors, tensors, pieces, tensors, pieces, tensors):
        scratch += [dma((n - 1,))] * 2
    spec = pl.BlockSpec(memory_space=pltpu.VMEM)
    results = (
        jax.ShapeDtypeStruct((users, beams), F32),
        jax.ShapeDtypeStruct((users, width), F32),
        jax.ShapeDtypeStruct((users, items), F32),
    )
    found = pl.pallas_call(
        functools.partial(kernel, cfg),
        out_shape=results,
        in_specs=[pl.BlockSpec(memory_space=pl.ANY)] * len(args),
        out_specs=(spec, spec, spec),
        scratch_shapes=scratch,
        compiler_params=pltpu.CompilerParams(
            collective_id=0, has_side_effects=True, vmem_limit_bytes=56 << 20
        ),
    )(*args)
    return pl.pallas_call(
        hand_over, out_shape=results,
        in_specs=[spec] * 3,
        out_specs=(spec,) * 3,
        compiler_params=pltpu.CompilerParams(vmem_limit_bytes=56 << 20),
    )(*found)


def solution(mesh):
    placed = (
        P("user", None),
        P("user", BOTH),
        P("user", "leaf"),
        P(),
        P(BOTH, None),
        P(BOTH, None),
        P(),
        P(),
        P(),
        P(),
        P(None, "tensor"),
        P(None, None, "tensor"),
        P(None, "tensor"),
        P("tensor"),
    )
    return jax.shard_map(
        per_device,
        mesh=mesh,
        in_specs=placed,
        out_specs=(P("user", BOTH), P("user", None), P("user", "leaf")),
        check_vma=False,
    )
```
